32 devices in a mesh: gx: 8 (over z, y), gy: 4 (over x, core).
Axes of the slice: x: 2, y: 2, z: 4, core: 2. Of those that a mesh axis runs over, the one named last changes fastest.
Arguments:
- spectra: bfloat16 [64, 128, 2048], P('gx', 'gy'), may hold values from -48 to 48
- resample_index: int32 [2048], replicated, may hold values from 0 to 2046
- resample_weight: float32 [2048], replicated, may hold values from 0 to 1
- disp_phase: float32 [2048], replicated, may hold values from -3.140625 to 3.140625
- surface_block: int32 [64, 128], P('gx', 'gy'), may hold values from 0 to 3
Outputs:
- enface: float32 [640, 64, 128], P(('gx', 'gy'))
The draws below stay inside these ranges and needn't reach their ends.
All inputs are finite; a program needn't handle non-finite values.
Results may differ from the reference program's by a relative error of at most 0.003.
Values sent between devices are 32-bit elements; how exact they have to be, the bound alone decides.
No kernel may reach another device: no remote copies, remote signals or barrier semaphores. Data moves between devices by JAX's collectives and lax.ppermute only.
A program may use at most 64 MiB of HBM per device.

```python
import math
import jax
import jax.numpy as jnp
from jax import lax

NK = 2048
BLOCK = 128
KEEP = 5
NX = 64
NY = 128


def draw_spectra(key, part):
    base_key = jax.random.fold_in(key, 11)
    first, second = jax.random.split(base_key, 2)
    position = jnp.arange(NX, dtype=jnp.float32) / max(NX - 1, 1)
    ramp = jnp.power(3.0, position)
    scales = jnp.exp(jax.random.uniform(second, (NX, NY), minval=0.0, maxval=jnp.log(10.0) / 2.0))
    noise = jax.random.normal(first, (NX, NY, NK))
    values = noise * ramp[:, None, None] * scales[:, :, None]
    return jnp.clip(values, -48.0, 48.0).astype(jnp.bfloat16)


def draw_resample_index(key, part):
    base_key = jax.random.fold_in(key, 23)
    jitter = jax.random.randint(base_key, (NK,), -3, 4)
    steps = jnp.arange(NK, dtype=jnp.int32)
    target = steps * (NK + 64) // NK + jitter
    return jnp.clip(target, 0, NK - 2).astype(jnp.int32)


def draw_surface_block(key, part):
    base_key = jax.random.fold_in(key, 37)
    first, second = jax.random.split(base_key, 2)
    span = NK // (2 * BLOCK) - KEEP
    tilt = jax.random.randint(first, (), span, 2 * span + 1)
    bump = jax.random.randint(second, (NX, NY), 0, 2)
    across = jnp.arange(NX, dtype=jnp.int32)[:, None]
    return jnp.minimum(span, tilt * across // NX + bump).astype(jnp.int32)


def setup_inputs(seed: int = 0) -> dict:
    splits = jax.random.split(jax.random.key(seed), 6)
    spectra = draw_spectra(jax.random.fold_in(splits[5], 71), 0)
    resample_index = draw_resample_index(jax.random.fold_in(splits[5], 71), 0)
    resample_weight = jnp.clip(jax.random.uniform(splits[2], (NK,), jnp.float32, 0.0, 1.0), 0.0, 1.0)
    disp_phase = jnp.clip(jax.random.uniform(splits[3], (NK,), jnp.float32, -3.140625, 3.140625), -3.140625, 3.140625)
    surface_block = draw_surface_block(jax.random.fold_in(splits[5], 71), 0)
    return dict(spectra=spectra, resample_index=resample_index, resample_weight=resample_weight, disp_phase=disp_phase, surface_block=surface_block)


def dft_table(samples, block):
    depths = samples // 2
    blocks = depths // block
    rows = jnp.arange(samples, dtype=jnp.int32)
    cols = jnp.arange(depths, dtype=jnp.int32)
    turns = ((rows[:, None] * cols[None, :]) % samples).astype(jnp.float32)
    angle = (2.0 * math.pi / samples) * turns
    cosine = jnp.cos(angle).astype(jnp.bfloat16).reshape(samples, blocks, block)
    sine = jnp.sin(angle).astype(jnp.bfloat16).reshape(samples, blocks, block)
    upper = jnp.concatenate([cosine, -sine], axis=2)
    lower = jnp.concatenate([sine, cosine], axis=2)
    return jnp.concatenate([upper, lower], axis=0)


def phase_planes(lines, resample_index, resample_weight, disp_phase):
    left = jnp.take(lines, resample_index, axis=1).astype(jnp.float32)
    right = jnp.take(lines, resample_index + 1, axis=1).astype(jnp.float32)
    resampled = (1.0 - resample_weight) * left + resample_weight * right
    real_part = (resampled * jnp.cos(disp_phase)).astype(jnp.bfloat16)
    imag_part = (resampled * jnp.sin(disp_phase)).astype(jnp.bfloat16)
    return jnp.concatenate([real_part, imag_part], axis=1)


def reference(spectra, resample_index, resample_weight, disp_phase, surface_block):
    blocks = NK // (2 * BLOCK)
    table = dft_table(NK, BLOCK).reshape(2 * NK, blocks * 2 * BLOCK)

    def one_line(operand):
        lines, surface = operand
        count = lines.shape[0]
        stacked = phase_planes(lines, resample_index, resample_weight, disp_phase)
        depth = jnp.dot(stacked, table, preferred_element_type=jnp.float32).reshape(count, blocks, 2, BLOCK)
        power = depth[:, :, 0] * depth[:, :, 0] + depth[:, :, 1] * depth[:, :, 1]
        picked = surface[:, None] + jnp.arange(KEEP, dtype=jnp.int32)[None, :]
        picked = jnp.broadcast_to(picked[:, :, None], (count, KEEP, BLOCK))
        kept = jnp.take_along_axis(power, picked, axis=1)
        return kept.reshape(count, KEEP * BLOCK)

    flat = lax.map(one_line, (spectra, surface_block))
    level = jnp.sum(flat) / (NX * NY * KEEP * BLOCK) + 1e-6
    image = jnp.log1p(flat / level)
    return jnp.transpose(image, (2, 0, 1))
```

```python
import functools
import math

import jax
import jax.numpy as jnp
from jax import lax
from jax.experimental import pallas as pl
from jax.experimental.pallas import tpu as pltpu
from jax.sharding import PartitionSpec as P

BLOCK = 128
KEEP = 5
LANES = 128
RADIX = 4
WINDOW = 512
JBLOCK = 256
NT = (((1,), (1,)), ((), ()))


def unit_circle(turns, samples):
    x = (turns - samples // 2).astype(jnp.float32) * (2.0 * math.pi / samples)
    s = x * x
    cosine = jnp.full_like(x, 1.0 / math.factorial(18))
    sine = jnp.full_like(x, 1.0 / math.factorial(19))
    for k in range(8, -1, -1):
        cosine = 1.0 / math.factorial(2 * k) - s * cosine
        sine = 1.0 / math.factorial(2 * k + 1) - s * sine
    return -cosine, -sine * x


def local_kernel(
    spec_ref, idx_ref, w_ref, cos_ref, sin_ref, surf_ref, out_ref,
    table, res, fold, flat, *, devices, rows, message,
):
    count, samples = spec_ref.shape
    short = samples // RADIX
    depths = samples // 2
    terms = depths // RADIX
    per_block = BLOCK // RADIX
    blocks = depths // BLOCK

    sub = lax.broadcasted_iota(jnp.int32, (8, short), 0)
    lane = lax.broadcasted_iota(jnp.int32, (8, short), 1)
    mask = samples - 1
    bases = [
        unit_circle(((RADIX * sub + q) * lane) & mask, samples) for q in range(RADIX)
    ]
    for g8 in range(terms // 64):
        rot_c, rot_s = unit_circle((8 * RADIX * (8 * g8 + sub) * lane) & mask, samples)
        for k in range(0, 8, 2):
            for q in range(RADIX):
                bc, bs = bases[q]
                both = []
                for t in (k, k + 1):
                    rc, rs = rot_c[t : t + 1], rot_s[t : t + 1]
                    both.append((bc * rc - bs * rs, bs * rc + bc * rs))
                row = (8 * g8 + k) * 8
                table[q, row : row + 16, :short] = jnp.concatenate(
                    [both[0][0], both[1][0]], axis=0
                ).astype(jnp.bfloat16)
                table[q, row : row + 16, short:] = jnp.concatenate(
                    [both[0][1], both[1][1]], axis=0
                ).astype(jnp.bfloat16)

    def gathered(j0, k0):
        cols = pl.ds(j0, JBLOCK)
        source = lax.broadcasted_iota(jnp.int32, (WINDOW, JBLOCK), 0) + k0
        left_of = idx_ref[:, cols]
        lhs = spec_ref[:, pl.ds(k0, WINDOW)]
        pick_left = (source == left_of).astype(jnp.float32).astype(jnp.bfloat16)
        pick_right = (source == left_of + 1).astype(jnp.float32).astype(jnp.bfloat16)
        left = jnp.dot(lhs, pick_left, preferred_element_type=jnp.float32)
        right = jnp.dot(lhs, pick_right, preferred_element_type=jnp.float32)
        w = w_ref[:, cols]
        return (1.0 - w) * left + w * right

    starts, ends = [], []
    for b in range(samples // JBLOCK):
        here = idx_ref[:, b * JBLOCK : (b + 1) * JBLOCK]
        low = jnp.min(here)
        k0 = jnp.minimum((low // LANES) * LANES, samples - WINDOW)
        starts.append(pl.multiple_of(k0, LANES))
        ends.append(jnp.max(here) + 2)
    for b, k0 in enumerate(starts):
        res[:, b * JBLOCK : (b + 1) * JBLOCK] = gathered(b * JBLOCK, k0)

    for b in range(samples // JBLOCK):
        first = starts[b] + WINDOW

        @pl.when(first < ends[b])
        def _():
            def step(i, carry):
                k = pl.multiple_of(first + i * LANES, LANES)
                j0 = b * JBLOCK
                source = lax.broadcasted_iota(jnp.int32, (LANES, JBLOCK), 0) + k
                cols = pl.ds(j0, JBLOCK)
                left_of = idx_ref[:, cols]
                lhs = spec_ref[:, pl.ds(k, LANES)]
                pl_ = (source == left_of).astype(jnp.float32).astype(jnp.bfloat16)
                pr_ = (source == left_of + 1).astype(jnp.float32).astype(jnp.bfloat16)
                left = jnp.dot(lhs, pl_, preferred_element_type=jnp.float32)
                right = jnp.dot(lhs, pr_, preferred_element_type=jnp.float32)
                w = w_ref[:, cols]
                res[:, cols] = res[:, cols] + ((1.0 - w) * left + w * right)
                return carry

            lax.fori_loop(0, (ends[b] - first + LANES - 1) // LANES, step, 0)

    for j in range(0, short, LANES):
        re, im = [], []
        for p in range(RADIX):
            cols = slice(p * short + j, p * short + j + LANES)
            r = res[:, cols]
            re.append((r * cos_ref[:, cols]).astype(jnp.bfloat16).astype(jnp.float32))
            im.append((r * sin_ref[:, cols]).astype(jnp.bfloat16).astype(jnp.float32))
        ar, ai = re[0] + re[2], im[0] + im[2]
        br, bi = re[0] - re[2], im[0] - im[2]
        cr, ci = re[1] + re[3], im[1] + im[3]
        dr, di = re[1] - re[3], im[1] - im[3]
        folded = [
            (ar + cr, ai + ci),
            (br + di, bi - dr),
            (ar - cr, ai - ci),
            (br - di, bi + dr),
        ]
        for q, (yr, yi) in enumerate(folded):
            yr, yi = yr.astype(jnp.bfloat16), yi.astype(jnp.bfloat16)
            fold[q, :count, j : j + LANES] = yr
            fold[q, :count, short + j : short + j + LANES] = yi
            fold[q, count:, j : j + LANES] = yi
            fold[q, count:, short + j : short + j + LANES] = -yr

    surface = surf_ref[...]
    total = jnp.zeros((8, LANES), jnp.float32)
    chosen = [surface == s for s in range(1, blocks - KEEP + 1)]
    for q in range(RADIX):
        depth = lax.dot_general(
            table[q], fold[q], NT, preferred_element_type=jnp.float32
        )
        re, im = depth[:, :count], depth[:, count:]
        power = re * re + im * im
        for k in range(KEEP):
            kept = power[k * per_block : (k + 1) * per_block]
            for s, hit in enumerate(chosen, 1):
                there = power[(k + s) * per_block : (k + s + 1) * per_block]
                kept = jnp.where(hit, there, kept)
            for h in range(count // LANES):
                half = kept[:, h * LANES : (h + 1) * LANES]
                total = total + jnp.sum(half.reshape(per_block // 8, 8, LANES), axis=0)
                flat[h, pl.ds(k * BLOCK + q, per_block, stride=RADIX), :] = half

    partial = jnp.sum(total, axis=0, keepdims=True)
    halves = count // LANES
    for dest in range(devices):
        base = dest * message
        for h in range(halves):
            out_ref[base + h * rows : base + (h + 1) * rows, :] = flat[
                h, dest * rows : (dest + 1) * rows, :
            ]
        out_ref[base + halves * rows : base + halves * rows + 1, :] = partial


def place_kernel(
    in_ref, out_ref, *, width_x, width_y, rows, message, across, along, scale
):
    devices = width_x * width_y
    halves = across * along // LANES
    chunks = LANES // along
    height = width_x * across
    groups = width_y // chunks
    sums = in_ref[pl.ds(halves * rows, devices, stride=message), :]
    level = jnp.sum(sums) * scale + 1e-06
    lane = lax.broadcasted_iota(jnp.int32, (1, LANES), 1)
    for gx in range(width_x):
        for group in range(groups):
            for h in range(halves):
                for r0 in range(0, rows, 8):
                    size = min(8, rows - r0)
                    parts = []
                    for c in range(chunks):
                        src = gx * width_y + group * chunks + c
                        start = src * message + h * rows + r0
                        parts.append(in_ref[start : start + size, :])
                    bit = 1
                    while bit < chunks:
                        upper = (lane // along) & bit != 0
                        mixed = list(parts)
                        for c in range(chunks):
                            if c & bit:
                                continue
                            a, b = parts[c], parts[c | bit]
                            mixed[c] = jnp.where(
                                upper, pltpu.roll(b, bit * along, 1), a
                            )
                            mixed[c | bit] = jnp.where(
                                upper, b, pltpu.roll(a, LANES - bit * along, 1)
                            )
                        parts = mixed
                        bit *= 2
                    for a in range(chunks):
                        x = gx * across + h * chunks + a
                        at = ((r0 * height + x - x % 8) * groups + group * 8) + x % 8
                        out_ref[pl.ds(at, size, stride=height * groups), :] = jnp.log1p(
                            parts[a] / level
                        )


def on_device(spectra, resample_index, resample_weight, disp_phase, surface_block):
    across, along, samples = spectra.shape
    count = across * along
    width_x = lax.axis_size("gx")
    width_y = lax.axis_size("gy")
    devices = width_x * width_y
    rows = KEEP * BLOCK // devices
    halves = count // LANES
    message = halves * rows + 1
    short = samples // RADIX
    terms = samples // 2 // RADIX
    vmem = pl.BlockSpec(memory_space=pltpu.VMEM)
    row = lambda v: v.reshape(1, v.size)
    sent = pl.pallas_call(
        functools.partial(local_kernel, devices=devices, rows=rows, message=message),
        out_shape=jax.ShapeDtypeStruct((devices * message, LANES), jnp.float32),
        in_specs=[vmem] * 6,
        out_specs=vmem,
        scratch_shapes=[
            pltpu.VMEM((RADIX, terms, 2 * short), jnp.bfloat16),
            pltpu.VMEM((count, samples), jnp.float32),
            pltpu.VMEM((RADIX, 2 * count, 2 * short), jnp.bfloat16),
            pltpu.VMEM((halves, KEEP * BLOCK, LANES), jnp.float32),
        ],
        name="local",
    )(
        spectra.reshape(count, samples),
        row(resample_index),
        row(resample_weight),
        row(jnp.cos(disp_phase)),
        row(jnp.sin(disp_phase)),
        row(surface_block),
    )
    moved = lax.all_to_all(
        sent.reshape(devices, message, 1, LANES),
        ("gx", "gy"),
        split_axis=0,
        concat_axis=0,
        tiled=True,
    ).reshape(devices * message, LANES)
    height, width = width_x * across, width_y * along
    groups = width // LANES
    placed = pl.pallas_call(
        functools.partial(
            place_kernel,
            width_x=width_x,
            width_y=width_y,
            rows=rows,
            message=message,
            across=across,
            along=along,
            scale=1.0 / (count * KEEP * BLOCK * devices),
        ),
        out_shape=jax.ShapeDtypeStruct((rows * height * groups, LANES), jnp.float32),
        in_specs=[vmem],
        out_specs=vmem,
        name="place",
    )(moved)
    placed = placed.reshape(rows, height // 8, groups, 8, LANES)
    return jnp.transpose(placed, (0, 1, 3, 2, 4)).reshape(rows, height, width)


def solution(mesh):
    placed = (P("gx", "gy", None), P(), P(), P(), P("gx", "gy"))
    return jax.shard_map(
        on_device,
        mesh=mesh,
        in_specs=placed,
        out_specs=P(("gx", "gy"), None, None),
        check_vma=False,
    )
```

```python
import functools
import math

import jax
import jax.numpy as jnp
from jax import lax
from jax.experimental import pallas as pl
from jax.experimental.pallas import tpu as pltpu
from jax.sharding import PartitionSpec as P

BLOCK = 128
KEEP = 5
LANES = 128
RADIX = 4
WINDOW = 256
HALF = LANES // 2
LIMIT = 63 << 20
NT = (((1,), (1,)), ((), ()))


def circle(x):
    s = x * x
    cosine = jnp.full_like(x, 1.0 / math.factorial(18))
    sine = jnp.full_like(x, 1.0 / math.factorial(19))
    for k in range(8, -1, -1):
        cosine = 1.0 / math.factorial(2 * k) - s * cosine
        sine = 1.0 / math.factorial(2 * k + 1) - s * sine
    return cosine, sine * x


def unit_circle(turns, samples):
    x = (turns - samples // 2).astype(jnp.float32) * (2.0 * math.pi / samples)
    cosine, sine = circle(x)
    return -cosine, -sine


def local_kernel(
    spec_hbm, idx_hbm, w_hbm, phase_hbm, surf_hbm, out_ref,
    table, spec, idx, weight, phase, surf, real, imag, fold, flat, starts, sems,
    *, devices, rows, message,
):
    count, samples = spec_hbm.shape
    short = samples // RADIX
    depths = samples // 2
    terms = depths // RADIX
    per_block = BLOCK // RADIX
    blocks = depths // BLOCK
    pieces = samples // LANES
    halves = count // LANES

    small = [
        pltpu.make_async_copy(idx_hbm, idx, sems.at[0]),
        pltpu.make_async_copy(w_hbm, weight, sems.at[1]),
        pltpu.make_async_copy(phase_hbm, phase, sems.at[2]),
        pltpu.make_async_copy(surf_hbm, surf, sems.at[3]),
    ]
    large = pltpu.make_async_copy(spec_hbm, spec.at[0], sems.at[4])
    for copy in small:
        copy.start()
    large.start()

    sub = lax.broadcasted_iota(jnp.int32, (8, short), 0)
    lane = lax.broadcasted_iota(jnp.int32, (8, short), 1)
    mask = samples - 1
    bases = [
        unit_circle(((RADIX * sub + q) * lane) & mask, samples) for q in range(RADIX)
    ]
    for g8 in range(terms // 64):
        rot_c, rot_s = unit_circle((8 * RADIX * (8 * g8 + sub) * lane) & mask, samples)
        for k in range(0, 8, 2):
            for q in range(RADIX):
                bc, bs = bases[q]
                both = []
                for t in (k, k + 1):
                    rc, rs = rot_c[t : t + 1], rot_s[t : t + 1]
                    both.append((bc * rc - bs * rs, bs * rc + bc * rs))
                row = (8 * g8 + k) * 8
                table[q, row : row + 16, :short] = jnp.concatenate(
                    [both[0][0], both[1][0]], axis=0
                ).astype(jnp.bfloat16)
                table[q, row : row + 16, short:] = jnp.concatenate(
                    [both[0][1], both[1][1]], axis=0
                ).astype(jnp.bfloat16)

    for copy in small:
        copy.wait()
    index = idx[...]
    low = jnp.min(index, axis=1, keepdims=True)
    first = jnp.minimum((low // HALF) * HALF, samples - WINDOW)
    high = jnp.max(index, axis=1, keepdims=True) + 2
    missed = jnp.max(high - first) > WINDOW
    steps = (high - first + (LANES - 1)) // LANES
    cos_phase, sin_phase = circle(phase[...])
    ws = weight[...]
    large.wait()
    spec[1, :, : samples - HALF] = spec[0, :, HALF:]
    spec[1, :, samples - HALF :] = jnp.zeros((count, HALF), spec.dtype)

    source = lax.broadcasted_iota(jnp.int32, (WINDOW, LANES), 0).astype(jnp.bfloat16)

    def pick(near):
        hits = []
        for k in range(2):
            want = jnp.clip(near + k, -1, WINDOW).astype(jnp.bfloat16)
            hits.append(jnp.where(source == want, jnp.bfloat16(1), jnp.bfloat16(0)))
        return jnp.concatenate(hits, axis=1)

    def finish(pair, w, c, s):
        r = (1.0 - w) * pair[:, :LANES] + w * pair[:, LANES:]
        return (r * c).astype(jnp.bfloat16), (r * s).astype(jnp.bfloat16)

    def window(k0):
        odd = (k0 // HALF) & 1
        at = pl.multiple_of(k0 - odd * HALF, LANES)
        return spec[odd, :, pl.ds(at, WINDOW)]

    for b in range(pieces):
        k0 = first[b, 0]
        row = slice(b, b + 1)
        near = index[row] - first[row]
        pair = jnp.dot(window(k0), pick(near), preferred_element_type=jnp.float32)
        real[b], imag[b] = finish(pair, ws[row], cos_phase[row], sin_phase[row])

    @pl.when(missed)
    def _():
        for b in range(pieces):
            starts[b] = first[b, 0]
            starts[pieces + b] = steps[b, 0]

        def redo(b, carry):
            @pl.when(starts[pieces + b] * LANES > WINDOW)
            def _():
                near = idx[pl.ds(b, 1), :]

                def step(i, pair):
                    k = starts[b] + i * LANES
                    odd = (k // HALF) & 1
                    at = pl.multiple_of(k - odd * HALF, LANES)
                    lines = spec[odd, :, pl.ds(at, LANES)]
                    hits = pick(near - k)[:LANES]
                    return pair + jnp.dot(
                        lines, hits, preferred_element_type=jnp.float32
                    )

                pair = lax.fori_loop(
                    0,
                    starts[pieces + b],
                    step,
                    jnp.zeros((count, 2 * LANES), jnp.float32),
                )
                c, s = circle(phase[pl.ds(b, 1), :])
                re, im = finish(pair, weight[pl.ds(b, 1), :], c, s)
                real[b] = re
                imag[b] = im

            return carry

        lax.fori_loop(0, pieces, redo, 0)

    lines_at = [surf[x : x + 1, :] for x in range(surf.shape[0])]
    per_half = LANES // surf.shape[1]
    quarter = pieces // RADIX
    total = jnp.zeros((8, LANES), jnp.float32)

    @pl.loop(0, count // 16)
    def _(chunk):
        top = pl.ds(pl.multiple_of(chunk * 16, 16), 16)
        bottom = pl.ds(pl.multiple_of(count + chunk * 16, 16), 16)
        for j in range(quarter):
            re, im = [], []
            for p in range(RADIX):
                re.append(real[p * quarter + j, top].astype(jnp.float32))
                im.append(imag[p * quarter + j, top].astype(jnp.float32))
            ar, ai = re[0] + re[2], im[0] + im[2]
            br, bi = re[0] - re[2], im[0] - im[2]
            cr, ci = re[1] + re[3], im[1] + im[3]
            dr, di = re[1] - re[3], im[1] - im[3]
            folded = [
                (ar + cr, ai + ci),
                (br + di, bi - dr),
                (ar - cr, ai - ci),
                (br - di, bi + dr),
            ]
            left = slice(j * LANES, (j + 1) * LANES)
            right = slice(short + j * LANES, short + (j + 1) * LANES)
            for q, (yr, yi) in enumerate(folded):
                yr, yi = yr.astype(jnp.bfloat16), yi.astype(jnp.bfloat16)
                fold[q, top, left] = yr
                fold[q, top, right] = yi
                fold[q, bottom, left] = yi
                fold[q, bottom, right] = -yr

    surface = [
        jnp.concatenate(lines_at[h * per_half : (h + 1) * per_half], axis=1)
        for h in range(halves)
    ]
    surface = jnp.concatenate(surface, axis=1)
    chosen = [surface == s for s in range(1, blocks - KEEP + 1)]
    for q in range(RADIX):
        depth = lax.dot_general(
            table[q], fold[q], NT, preferred_element_type=jnp.float32
        )
        re, im = depth[:, :count], depth[:, count:]
        power = re * re + im * im
        for k in range(KEEP):
            kept = power[k * per_block : (k + 1) * per_block]
            for s, hit in enumerate(chosen, 1):
                there = power[(k + s) * per_block : (k + s + 1) * per_block]
                kept = jnp.where(hit, there, kept)
            base = q * (KEEP * per_block) + k * per_block
            for h in range(halves):
                half = kept[:, h * LANES : (h + 1) * LANES]
                total = total + jnp.sum(half.reshape(per_block // 8, 8, LANES), axis=0)
                flat[h, base : base + per_block, :] = half
    for h in range(halves):
        for m in range(KEEP * per_block):
            four = flat[h, pl.ds(m, RADIX, stride=KEEP * per_block), :]
            r = RADIX * m
            while r < RADIX * (m + 1):
                dest = r // rows
                stop = min(RADIX * (m + 1), (dest + 1) * rows)
                at = dest * message + h * rows + r % rows
                out_ref[at : at + stop - r, :] = four[
                    r - RADIX * m : stop - RADIX * m
                ]
                r = stop

    partial = jnp.sum(total, axis=0, keepdims=True)
    for dest in range(devices):
        at = dest * message + halves * rows
        out_ref[at : at + 1, :] = partial


def place_kernel(
    in_ref, out_hbm, stage, sem, *, width_x, width_y, rows, message, across, along, scale
):
    devices = width_x * width_y
    halves = across * along // LANES
    chunks = LANES // along
    groups = width_y // chunks
    sums = in_ref[pl.ds(halves * rows, devices, stride=message), :]
    inverse = 1.0 / (jnp.sum(sums) * scale + 1e-06)
    lane = lax.broadcasted_iota(jnp.int32, (1, LANES), 1)
    copies = []
    for gx in range(width_x):
        for group in range(groups):
            for h in range(halves):
                for r0 in range(0, rows, 8):
                    size = min(8, rows - r0)
                    parts = []
                    for c in range(chunks):
                        src = gx * width_y + group * chunks + c
                        start = src * message + h * rows + r0
                        parts.append(
                            jnp.log(1.0 + in_ref[start : start + size, :] * inverse)
                        )
                    bit = 1
                    while bit < chunks:
                        upper = (lane // along) & bit != 0
                        mixed = list(parts)
                        for c in range(chunks):
                            if c & bit:
                                continue
                            a, b = parts[c], parts[c | bit]
                            if 2 * bit == chunks:
                                up = down = pltpu.roll(
                                    jnp.where(upper, a, b), LANES // 2, 1
                                )
                            else:
                                up = pltpu.roll(b, bit * along, 1)
                                down = pltpu.roll(a, LANES - bit * along, 1)
                            mixed[c] = jnp.where(upper, up, a)
                            mixed[c | bit] = jnp.where(upper, b, down)
                        parts = mixed
                        bit *= 2
                    for a in range(chunks):
                        at = (gx * across + h * chunks + a) * groups + group
                        stage[at, r0 : r0 + size, :] = parts[a]
                for a in range(chunks):
                    x = gx * across + h * chunks + a
                    copy = pltpu.make_async_copy(
                        stage.at[x * groups + group],
                        out_hbm.at[:, x // 8, group, x % 8],
                        sem.at[x * groups + group],
                    )
                    copy.start()
                    copies.append(copy)
    for copy in copies:
        copy.wait()


def on_device(spectra, resample_index, resample_weight, disp_phase, surface_block):
    across, along, samples = spectra.shape
    count = across * along
    width_x = lax.axis_size("gx")
    width_y = lax.axis_size("gy")
    devices = width_x * width_y
    rows = KEEP * BLOCK // devices
    halves = count // LANES
    message = halves * rows + 1
    short = samples // RADIX
    terms = samples // 2 // RADIX
    pieces = samples // LANES
    vmem = pl.BlockSpec(memory_space=pltpu.VMEM)
    hbm = pl.BlockSpec(memory_space=pltpu.HBM)
    sent = pl.pallas_call(
        functools.partial(local_kernel, devices=devices, rows=rows, message=message),
        out_shape=jax.ShapeDtypeStruct((devices * message, LANES), jnp.float32),
        in_specs=[hbm] * 5,
        out_specs=vmem,
        scratch_shapes=[
            pltpu.VMEM((RADIX, terms, 2 * short), jnp.bfloat16),
            pltpu.VMEM((2, count, samples), jnp.bfloat16),
            pltpu.VMEM((pieces, LANES), jnp.int32),
            pltpu.VMEM((pieces, LANES), jnp.float32),
            pltpu.VMEM((pieces, LANES), jnp.float32),
            pltpu.VMEM((across, along), jnp.int32),
            pltpu.VMEM((pieces, count, LANES), jnp.bfloat16),
            pltpu.VMEM((pieces, count, LANES), jnp.bfloat16),
            pltpu.VMEM((RADIX, 2 * count, 2 * short), jnp.bfloat16),
            pltpu.VMEM((halves, KEEP * BLOCK, LANES), jnp.float32),
            pltpu.SMEM((2 * pieces,), jnp.int32),
            pltpu.SemaphoreType.DMA((5,)),
        ],
        compiler_params=pltpu.CompilerParams(vmem_limit_bytes=LIMIT),
        name="local",
    )(
        spectra.reshape(count, samples),
        resample_index.reshape(pieces, LANES),
        resample_weight.reshape(pieces, LANES),
        disp_phase.reshape(pieces, LANES),
        surface_block,
    )
    moved = lax.all_to_all(
        sent.reshape(devices, message, 1, LANES),
        ("gx", "gy"),
        split_axis=0,
        concat_axis=0,
        tiled=True,
    ).reshape(devices * message, LANES)
    height, width = width_x * across, width_y * along
    groups = width // LANES
    placed = pl.pallas_call(
        functools.partial(
            place_kernel,
            width_x=width_x,
            width_y=width_y,
            rows=rows,
            message=message,
            across=across,
            along=along,
            scale=1.0 / (count * KEEP * BLOCK * devices),
        ),
        out_shape=jax.ShapeDtypeStruct(
            (rows, height // 8, groups, 8, LANES), jnp.float32
        ),
        in_specs=[vmem],
        out_specs=hbm,
        scratch_shapes=[
            pltpu.VMEM((height * groups, rows, LANES), jnp.float32),
            pltpu.SemaphoreType.DMA((height * groups,)),
        ],
        compiler_params=pltpu.CompilerParams(vmem_limit_bytes=8 << 20),
        name="place",
    )(moved)
    return jnp.transpose(placed, (0, 1, 3, 2, 4)).reshape(rows, height, width)


def solution(mesh):
    placed = (P("gx", "gy", None), P(), P(), P(), P("gx", "gy"))
    return jax.shard_map(
        on_device,
        mesh=mesh,
        in_specs=placed,
        out_specs=P(("gx", "gy"), None, None),
        check_vma=False,
    )
```

```python
import functools
import math

import jax
import jax.numpy as jnp
from jax import lax
from jax.experimental import pallas as pl
from jax.experimental.pallas import tpu as pltpu
from jax.sharding import PartitionSpec as P

BLOCK = 128
KEEP = 5
LANES = 128
RADIX = 4
WINDOW = 256
PAIR = 2
LIMIT = 63 << 20
NT = (((1,), (1,)), ((), ()))


def circle(x):
    s = x * x
    cosine = jnp.full_like(x, 1.0 / math.factorial(18))
    sine = jnp.full_like(x, 1.0 / math.factorial(19))
    for k in range(8, -1, -1):
        cosine = 1.0 / math.factorial(2 * k) - s * cosine
        sine = 1.0 / math.factorial(2 * k + 1) - s * sine
    return cosine, sine * x


def unit_circle(turns, samples):
    x = (turns - samples // 2).astype(jnp.float32) * (2.0 * math.pi / samples)
    cosine, sine = circle(x)
    return -cosine, -sine


def place_in_message(r, rows):
    if rows % RADIX:
        return r
    return (r % RADIX) * (rows // RADIX) + r // RADIX


def local_kernel(
    spec_hbm, idx_hbm, w_hbm, phase_hbm, surf_hbm, out_ref,
    table, spec, idx, weight, phase, surf, real, imag, fold, total, starts, sems,
    *, devices, rows, message,
):
    count, samples = spec_hbm.shape
    short = samples // RADIX
    depths = samples // 2
    terms = depths // RADIX
    per_block = BLOCK // RADIX
    blocks = depths // BLOCK
    pieces = samples // LANES
    quarter = pieces // RADIX
    halves = count // LANES

    small = [
        pltpu.make_async_copy(idx_hbm, idx, sems.at[0]),
        pltpu.make_async_copy(w_hbm, weight, sems.at[1]),
        pltpu.make_async_copy(phase_hbm, phase, sems.at[2]),
        pltpu.make_async_copy(surf_hbm, surf, sems.at[3]),
    ]
    large = pltpu.make_async_copy(spec_hbm, spec, sems.at[4])
    for copy in small:
        copy.start()
    large.start()

    sub = lax.broadcasted_iota(jnp.int32, (8, short), 0)
    lane = lax.broadcasted_iota(jnp.int32, (8, short), 1)
    mask = samples - 1
    bases = [
        unit_circle(((RADIX * sub + q) * lane) & mask, samples) for q in range(RADIX)
    ]
    for g8 in range(terms // 64):
        rot_c, rot_s = unit_circle((8 * RADIX * (8 * g8 + sub) * lane) & mask, samples)
        for k in range(0, 8, 2):
            for q in range(RADIX):
                bc, bs = bases[q]
                both = []
                for t in (k, k + 1):
                    rc, rs = rot_c[t : t + 1], rot_s[t : t + 1]
                    both.append((bc * rc - bs * rs, bs * rc + bc * rs))
                row = (8 * g8 + k) * 8
                table[q, row : row + 16, :short] = jnp.concatenate(
                    [both[0][0], both[1][0]], axis=0
                ).astype(jnp.bfloat16)
                table[q, row : row + 16, short:] = jnp.concatenate(
                    [both[0][1], both[1][1]], axis=0
                ).astype(jnp.bfloat16)
    total[...] = jnp.zeros_like(total)

    for copy in small:
        copy.wait()
    index = idx[...]
    low = jnp.min(index, axis=1, keepdims=True)
    first = jnp.minimum((low // LANES) * LANES, samples - WINDOW)
    high = jnp.max(index, axis=1, keepdims=True) + 2
    longest = jnp.max(high - first)
    steps = (high - first + (LANES - 1)) // LANES
    cos_phase, sin_phase = circle(phase[...])
    ws = weight[...]
    vs = 1.0 - ws
    near_all = index - first
    large.wait()

    source = lax.broadcasted_iota(jnp.int32, (WINDOW, LANES), 0).astype(jnp.bfloat16)

    def pick(near):
        hits = []
        for k in range(2):
            want = jnp.clip(near + k, -1, WINDOW).astype(jnp.bfloat16)
            hits.append(jnp.where(source == want, jnp.bfloat16(1), jnp.bfloat16(0)))
        return jnp.concatenate(hits, axis=1)

    def finish(pair, v, w, c, s):
        r = v * pair[:, :LANES] + w * pair[:, LANES:]
        return (r * c).astype(jnp.bfloat16), (r * s).astype(jnp.bfloat16)

    for b in range(pieces):
        row = slice(b, b + 1)
        lines = spec[:, pl.ds(pl.multiple_of(first[b, 0], LANES), WINDOW)]
        pair = jnp.dot(lines, pick(near_all[row]), preferred_element_type=jnp.float32)
        real[b], imag[b] = finish(pair, vs[row], ws[row], cos_phase[row], sin_phase[row])

    @pl.when(longest > WINDOW)
    def _():
        for b in range(pieces):
            starts[b] = first[b, 0]
            starts[pieces + b] = steps[b, 0]

        def redo(b, carry):
            @pl.when(starts[pieces + b] * LANES > WINDOW)
            def _():
                near = idx[pl.ds(b, 1), :]

                def step(i, pair):
                    k = pl.multiple_of(starts[b] + i * LANES, LANES)
                    hits = pick(near - k)[:LANES]
                    return pair + jnp.dot(
                        spec[:, pl.ds(k, LANES)],
                        hits,
                        preferred_element_type=jnp.float32,
                    )

                pair = lax.fori_loop(
                    0,
                    starts[pieces + b],
                    step,
                    jnp.zeros((count, 2 * LANES), jnp.float32),
                )
                c, s = circle(phase[pl.ds(b, 1), :])
                w = weight[pl.ds(b, 1), :]
                re, im = finish(pair, 1.0 - w, w, c, s)
                real[b] = re
                imag[b] = im

            return carry

        lax.fori_loop(0, pieces, redo, 0)

    def fold_lines(h, r0):
        at = pl.ds(pl.multiple_of(h * LANES + r0, 16), 16)
        top = pl.ds(pl.multiple_of(r0, 16), 16)
        bottom = pl.ds(pl.multiple_of(LANES + r0, 16), 16)
        for j in range(quarter):
            re, im = [], []
            for p in range(RADIX):
                re.append(real[p * quarter + j, at].astype(jnp.float32))
                im.append(imag[p * quarter + j, at].astype(jnp.float32))
            ar, ai = re[0] + re[2], im[0] + im[2]
            br, bi = re[0] - re[2], im[0] - im[2]
            cr, ci = re[1] + re[3], im[1] + im[3]
            dr, di = re[1] - re[3], im[1] - im[3]
            folded = [
                (ar + cr, ai + ci),
                (br + di, bi - dr),
                (ar - cr, ai - ci),
                (br - di, bi + dr),
            ]
            left = slice(j * LANES, (j + 1) * LANES)
            right = slice(short + j * LANES, short + (j + 1) * LANES)
            for q, (yr, yi) in enumerate(folded):
                yr, yi = yr.astype(jnp.bfloat16), yi.astype(jnp.bfloat16)
                fold[h, q, top, left] = yr
                fold[h, q, top, right] = yi
                fold[h, q, bottom, left] = yi
                fold[h, q, bottom, right] = -yr

    per_half = LANES // surf.shape[1]

    def transform(h, q):
        lines_at = range(h * per_half, (h + 1) * per_half)
        surface = jnp.concatenate([surf[x : x + 1, :] for x in lines_at], axis=1)
        chosen = [surface == s for s in range(1, blocks - KEEP + 1)]
        depth = lax.dot_general(
            table[q], fold[h, q], NT, preferred_element_type=jnp.float32
        )
        re, im = depth[:, :LANES], depth[:, LANES:]
        power = re * re + im * im
        for k in range(KEEP):
            kept = power[k * per_block : (k + 1) * per_block]
            for s, hit in enumerate(chosen, 1):
                there = power[(k + s) * per_block : (k + s + 1) * per_block]
                kept = jnp.where(hit, there, kept)
            total[...] += jnp.sum(kept.reshape(per_block // 8, 8, LANES), axis=0)
            places = []
            for m in range(per_block):
                r = (k * per_block + m) * RADIX + q
                inside = place_in_message(r % rows, rows)
                places.append((r // rows) * message + h * rows + inside)
            m = 0
            while m < per_block:
                stop = m + 1
                while stop % 8 and places[stop] == places[stop - 1] + 1:
                    stop += 1
                out_ref[places[m] : places[m] + stop - m, :] = kept[m:stop]
                m = stop

    @pl.loop(0, LANES // 32)
    def _(chunk):
        for part in range(2):
            fold_lines(0, chunk * 32 + part * 16)

    for h in range(halves):
        for q0 in range(0, RADIX, PAIR):

            @pl.when(longest > 0)
            def _():
                for q in range(q0, q0 + PAIR):
                    transform(h, q)
                if h + 1 < halves:
                    share = LANES * PAIR // RADIX
                    begin = q0 // PAIR * share
                    for r0 in range(begin, begin + share, 16):
                        fold_lines(h + 1, r0)

    partial = jnp.sum(total[...], axis=0, keepdims=True)
    for dest in range(devices):
        at = dest * message + halves * rows
        out_ref[at : at + 1, :] = partial


def swap_chunks(parts, along, lane):
    chunks = len(parts)
    bit = 1
    while bit < chunks:
        upper = (lane // along) & bit != 0
        mixed = list(parts)
        for c in range(chunks):
            if c & bit:
                continue
            a, b = parts[c], parts[c | bit]
            if 2 * bit == chunks:
                up = down = pltpu.roll(jnp.where(upper, a, b), LANES // 2, 1)
            else:
                up = pltpu.roll(b, bit * along, 1)
                down = pltpu.roll(a, LANES - bit * along, 1)
            mixed[c] = jnp.where(upper, up, a)
            mixed[c | bit] = jnp.where(upper, b, down)
        parts = mixed
        bit *= 2
    return parts


def place_kernel(
    in_ref, out_hbm, stage, sem, *, width_x, width_y, rows, message, across, along, scale
):
    devices = width_x * width_y
    halves = across * along // LANES
    chunks = LANES // along
    groups = width_y // chunks
    sums = in_ref[pl.ds(halves * rows, devices, stride=message), :]
    inverse = 1.0 / (jnp.sum(sums) * scale + 1e-06)
    lane = lax.broadcasted_iota(jnp.int32, (1, LANES), 1)
    outer, inner = stage.shape[2], stage.shape[4]

    for gx in range(width_x):
        for group in range(groups):
            at = gx * groups + group
            heads = [
                (gx * width_y + group * chunks + c) * message for c in range(chunks)
            ]
            for u in range(outer):
                if inner == RADIX:
                    blocks = [pl.ds(head + u, halves * inner, stride=outer) for head in heads]
                    blocks = [jnp.log(1.0 + in_ref[b, :] * inverse) for b in blocks]
                    blocks = swap_chunks(blocks, along, lane)
                    for a in range(chunks):
                        for h in range(halves):
                            stage[at, a, u, h] = blocks[a][h * inner : (h + 1) * inner]
                else:
                    for h in range(halves):
                        blocks = [pl.ds(head + h * rows + u * inner, inner) for head in heads]
                        blocks = [jnp.log(1.0 + in_ref[b, :] * inverse) for b in blocks]
                        blocks = swap_chunks(blocks, along, lane)
                        for a in range(chunks):
                            stage[at, a, u, h] = blocks[a]
            for h in range(halves):
                for a in range(chunks):
                    x = gx * across + h * chunks + a
                    pltpu.make_async_copy(
                        stage.at[at, a, :, h],
                        out_hbm.at[:, :, x // 8, group, x % 8],
                        sem,
                    ).start()
    pltpu.make_async_copy(stage, stage, sem).wait()


def on_device(spectra, resample_index, resample_weight, disp_phase, surface_block):
    across, along, samples = spectra.shape
    count = across * along
    width_x = lax.axis_size("gx")
    width_y = lax.axis_size("gy")
    devices = width_x * width_y
    rows = KEEP * BLOCK // devices
    halves = count // LANES
    message = halves * rows + 1
    short = samples // RADIX
    terms = samples // 2 // RADIX
    pieces = samples // LANES
    vmem = pl.BlockSpec(memory_space=pltpu.VMEM)
    hbm = pl.BlockSpec(memory_space=pltpu.HBM)
    sent = pl.pallas_call(
        functools.partial(local_kernel, devices=devices, rows=rows, message=message),
        out_shape=jax.ShapeDtypeStruct((devices * message, LANES), jnp.float32),
        in_specs=[hbm] * 5,
        out_specs=vmem,
        scratch_shapes=[
            pltpu.VMEM((RADIX, terms, 2 * short), jnp.bfloat16),
            pltpu.VMEM((count, samples), jnp.bfloat16),
            pltpu.VMEM((pieces, LANES), jnp.int32),
            pltpu.VMEM((pieces, LANES), jnp.float32),
            pltpu.VMEM((pieces, LANES), jnp.float32),
            pltpu.VMEM((across, along), jnp.int32),
            pltpu.VMEM((pieces, count, LANES), jnp.bfloat16),
            pltpu.VMEM((pieces, count, LANES), jnp.bfloat16),
            pltpu.VMEM((halves, RADIX, 2 * LANES, 2 * short), jnp.bfloat16),
            pltpu.VMEM((8, LANES), jnp.float32),
            pltpu.SMEM((2 * pieces,), jnp.int32),
            pltpu.SemaphoreType.DMA((5,)),
        ],
        compiler_params=pltpu.CompilerParams(vmem_limit_bytes=LIMIT),
        name="local",
    )(
        spectra.reshape(count, samples),
        resample_index.reshape(pieces, LANES),
        resample_weight.reshape(pieces, LANES),
        disp_phase.reshape(pieces, LANES),
        surface_block,
    )
    moved = lax.all_to_all(
        sent.reshape(devices, message, 1, LANES),
        ("gx", "gy"),
        split_axis=0,
        concat_axis=0,
        tiled=True,
    ).reshape(devices * message, LANES)
    height, width = width_x * across, width_y * along
    groups = width // LANES
    inner = rows if rows % RADIX else RADIX
    placed = pl.pallas_call(
        functools.partial(
            place_kernel,
            width_x=width_x,
            width_y=width_y,
            rows=rows,
            message=message,
            across=across,
            along=along,
            scale=1.0 / (count * KEEP * BLOCK * devices),
        ),
        out_shape=jax.ShapeDtypeStruct(
            (rows // inner, inner, height // 8, groups, 8, LANES), jnp.float32
        ),
        in_specs=[vmem],
        out_specs=hbm,
        scratch_shapes=[
            pltpu.VMEM(
                (width_x * groups, LANES // along, rows // inner, halves, inner, LANES),
                jnp.float32,
            ),
            pltpu.SemaphoreType.DMA,
        ],
        compiler_params=pltpu.CompilerParams(vmem_limit_bytes=8 << 20),
        name="place",
    )(moved)
    placed = placed.reshape(rows, height // 8, groups, 8, LANES)
    return jnp.transpose(placed, (0, 1, 3, 2, 4)).reshape(rows, height, width)


def solution(mesh):
    placed = (P("gx", "gy", None), P(), P(), P(), P("gx", "gy"))
    return jax.shard_map(
        on_device,
        mesh=mesh,
        in_specs=placed,
        out_specs=P(("gx", "gy"), None, None),
        check_vma=False,
    )
```

```python
import functools
import math

import jax
import jax.numpy as jnp
from jax import lax
from jax.experimental import pallas as pl
from jax.experimental.pallas import tpu as pltpu
from jax.sharding import PartitionSpec as P

BLOCK = 128
KEEP = 5
LANES = 128
RADIX = 4
WINDOW = 256
PAIR = 2
BATCH = 4
LIMIT = 63 << 20
NT = (((1,), (1,)), ((), ()))


def circle(x):
    s = x * x
    cosine = jnp.full_like(x, 1.0 / math.factorial(18))
    sine = jnp.full_like(x, 1.0 / math.factorial(19))
    for k in range(8, -1, -1):
        cosine = 1.0 / math.factorial(2 * k) - s * cosine
        sine = 1.0 / math.factorial(2 * k + 1) - s * sine
    return cosine, sine * x


def unit_circle(turns, samples):
    x = (turns - samples // 2).astype(jnp.float32) * (2.0 * math.pi / samples)
    cosine, sine = circle(x)
    return -cosine, -sine


def place_in_message(r, rows):
    if rows % RADIX:
        return r
    return (r % RADIX) * (rows // RADIX) + r // RADIX


def local_kernel(
    spec_hbm, idx_hbm, w_hbm, phase_hbm, surf_hbm, out_ref,
    table, spec, idx, weight, phase, surf, real, imag, fold, total, starts, sems,
    *, devices, rows, message,
):
    count, samples = spec_hbm.shape
    short = samples // RADIX
    depths = samples // 2
    terms = depths // RADIX
    per_block = BLOCK // RADIX
    blocks = depths // BLOCK
    pieces = samples // LANES
    quarter = pieces // RADIX
    halves = count // LANES

    small = [
        pltpu.make_async_copy(idx_hbm, idx, sems.at[0]),
        pltpu.make_async_copy(w_hbm, weight, sems.at[1]),
        pltpu.make_async_copy(phase_hbm, phase, sems.at[2]),
        pltpu.make_async_copy(surf_hbm, surf, sems.at[3]),
    ]
    large = pltpu.make_async_copy(spec_hbm, spec, sems.at[4])
    for copy in small:
        copy.start()
    large.start()

    sub = lax.broadcasted_iota(jnp.int32, (8, short // 2), 0)
    lane = 2 * lax.broadcasted_iota(jnp.int32, (8, short // 2), 1) + 1
    turn = 2 * samples
    bases = [
        unit_circle(((RADIX * sub + q) * lane) & (turn - 1), turn) for q in range(RADIX)
    ]
    for g8 in range(terms // 64):
        rot_c, rot_s = unit_circle((8 * RADIX * (8 * g8 + sub) * lane) & (turn - 1), turn)
        for k in range(0, 8, 2):
            for q in range(RADIX):
                bc, bs = bases[q]
                both = []
                for t in (k, k + 1):
                    rc, rs = rot_c[t : t + 1], rot_s[t : t + 1]
                    both.append((bc * rc - bs * rs, bs * rc + bc * rs))
                row = (8 * g8 + k) * 8
                table[q, row : row + 16, : short // 2] = jnp.concatenate(
                    [both[0][0], both[1][0]], axis=0
                ).astype(jnp.bfloat16)
                table[q, row : row + 16, short // 2 :] = jnp.concatenate(
                    [both[0][1], both[1][1]], axis=0
                ).astype(jnp.bfloat16)
    total[...] = jnp.zeros_like(total)

    for copy in small:
        copy.wait()
    piece = lax.broadcasted_iota(jnp.int32, idx.shape, 0)
    back = LANES - 1 - lax.broadcasted_iota(jnp.int32, idx.shape, 1)

    def mirrored(ref):
        v = ref[...]
        turned = jnp.take_along_axis(v, back, axis=1, mode="promise_in_bounds")
        return jnp.where(piece % quarter >= quarter // 2, turned, v)

    index = mirrored(idx)
    idx[...] = index
    low = jnp.min(index, axis=1, keepdims=True)
    first = jnp.minimum((low // LANES) * LANES, samples - WINDOW)
    high = jnp.max(index, axis=1, keepdims=True) + 2
    longest = jnp.max(high - first)
    steps = (high - first + (LANES - 1)) // LANES
    phases = mirrored(phase)
    phase[...] = phases
    cos_phase, sin_phase = circle(phases)
    ws = mirrored(weight)
    weight[...] = ws
    vs = 1.0 - ws
    near_all = index - first
    large.wait()

    source = lax.broadcasted_iota(jnp.int32, (WINDOW, LANES), 0).astype(jnp.bfloat16)

    def pick(near):
        hits = []
        for k in range(2):
            want = jnp.clip(near + k, -1, WINDOW).astype(jnp.bfloat16)
            hits.append(jnp.where(source == want, jnp.bfloat16(1), jnp.bfloat16(0)))
        return jnp.concatenate(hits, axis=1)

    def finish(pair, v, w, c, s):
        r = v * pair[:, :LANES] + w * pair[:, LANES:]
        return (r * c).astype(jnp.bfloat16), (r * s).astype(jnp.bfloat16)

    for b in range(pieces):
        row = slice(b, b + 1)
        lines = spec[:, pl.ds(pl.multiple_of(first[b, 0], LANES), WINDOW)]
        pair = jnp.dot(lines, pick(near_all[row]), preferred_element_type=jnp.float32)
        real[b], imag[b] = finish(pair, vs[row], ws[row], cos_phase[row], sin_phase[row])

    @pl.when(longest > WINDOW)
    def _():
        for b in range(pieces):
            starts[b] = first[b, 0]
            starts[pieces + b] = steps[b, 0]

        def redo(b, carry):
            @pl.when(starts[pieces + b] * LANES > WINDOW)
            def _():
                near = idx[pl.ds(b, 1), :]

                def step(i, pair):
                    k = pl.multiple_of(starts[b] + i * LANES, LANES)
                    hits = pick(near - k)[:LANES]
                    return pair + jnp.dot(
                        spec[:, pl.ds(k, LANES)],
                        hits,
                        preferred_element_type=jnp.float32,
                    )

                pair = lax.fori_loop(
                    0,
                    starts[pieces + b],
                    step,
                    jnp.zeros((count, 2 * LANES), jnp.float32),
                )
                c, s = circle(phase[pl.ds(b, 1), :])
                w = weight[pl.ds(b, 1), :]
                re, im = finish(pair, 1.0 - w, w, c, s)
                real[b] = re
                imag[b] = im

            return carry

        lax.fori_loop(0, pieces, redo, 0)

    def fold_lines(h, r0):
        at = pl.ds(pl.multiple_of(h * LANES + r0, 16), 16)
        top = pl.ds(pl.multiple_of(r0, 16), 16)
        bottom = pl.ds(pl.multiple_of(LANES + r0, 16), 16)
        for t in range(quarter // 2):
            re, im, re_, im_ = [], [], [], []
            for p in range(RADIX):
                re.append(real[p * quarter + t, at].astype(jnp.float32))
                im.append(imag[p * quarter + t, at].astype(jnp.float32))
                u = (p + 1) * quarter - 1 - t
                re_.append(real[u, at].astype(jnp.float32))
                im_.append(imag[u, at].astype(jnp.float32))
            ar, ai = re[0] + re[2], im[0] + im[2]
            br, bi = re[0] - re[2], im[0] - im[2]
            cr, ci = re[1] + re[3], im[1] + im[3]
            dr, di = re[1] - re[3], im[1] - im[3]
            ar_, ai_ = re_[0] + re_[2], im_[0] + im_[2]
            br_, bi_ = re_[0] - re_[2], im_[0] - im_[2]
            cr_, ci_ = re_[1] + re_[3], im_[1] + im_[3]
            er_, di_ = re_[3] - re_[1], im_[1] - im_[3]
            yz = [
                (ar + cr, ai + ci, ar_ + cr_, ai_ + ci_, True),
                (br + di, bi - dr, bi_ + er_, br_ + di_, False),
                (ar - cr, ai - ci, cr_ - ar_, ci_ - ai_, True),
                (br - di, bi + dr, er_ - bi_, br_ - di_, True),
            ]
            left = slice(t * LANES, (t + 1) * LANES)
            right = slice(short // 2 + t * LANES, short // 2 + (t + 1) * LANES)
            for q, (yr, yi, zr, zi, plus) in enumerate(yz):
                even, odd = (yi + zi, yi - zi) if plus else (yi - zi, yi + zi)
                fold[h, q, top, left] = (yr + zr).astype(jnp.bfloat16)
                fold[h, q, top, right] = odd.astype(jnp.bfloat16)
                fold[h, q, bottom, left] = even.astype(jnp.bfloat16)
                fold[h, q, bottom, right] = (zr - yr).astype(jnp.bfloat16)

    per_half = LANES // surf.shape[1]

    def transform(h, q):
        lines_at = range(h * per_half, (h + 1) * per_half)
        surface = jnp.concatenate([surf[x : x + 1, :] for x in lines_at], axis=1)
        chosen = [surface == s for s in range(1, blocks - KEEP + 1)]
        depth = lax.dot_general(
            table[q], fold[h, q], NT, preferred_element_type=jnp.float32
        )
        re, im = depth[:, :LANES], depth[:, LANES:]
        power = re * re + im * im
        for k in range(KEEP):
            kept = power[k * per_block : (k + 1) * per_block]
            for s, hit in enumerate(chosen, 1):
                there = power[(k + s) * per_block : (k + s + 1) * per_block]
                kept = jnp.where(hit, there, kept)
            total[...] += jnp.sum(kept.reshape(per_block // 8, 8, LANES), axis=0)
            places = []
            for m in range(per_block):
                r = (k * per_block + m) * RADIX + q
                inside = place_in_message(r % rows, rows)
                places.append((r // rows) * message + h * rows + inside)
            m = 0
            while m < per_block:
                stop = m + 1
                while stop % 8 and places[stop] == places[stop - 1] + 1:
                    stop += 1
                out_ref[places[m] : places[m] + stop - m, :] = kept[m:stop]
                m = stop

    @pl.loop(0, LANES // 32)
    def _(chunk):
        for part in range(2):
            fold_lines(0, chunk * 32 + part * 16)

    for h in range(halves):
        for q0 in range(0, RADIX, PAIR):

            @pl.when(longest > 0)
            def _():
                for q in range(q0, q0 + PAIR):
                    transform(h, q)
                if h + 1 < halves:
                    share = LANES * PAIR // RADIX
                    begin = q0 // PAIR * share
                    for r0 in range(begin, begin + share, 16):
                        fold_lines(h + 1, r0)

    partial = jnp.sum(total[...], axis=0, keepdims=True)
    for dest in range(devices):
        at = dest * message + halves * rows
        out_ref[at : at + 1, :] = partial


def swap_chunks(parts, along, lane):
    chunks = len(parts)
    bit = 1
    while bit < chunks:
        upper = (lane // along) & bit != 0
        mixed = list(parts)
        for c in range(chunks):
            if c & bit:
                continue
            a, b = parts[c], parts[c | bit]
            if 2 * bit == chunks:
                up = down = pltpu.roll(jnp.where(upper, a, b), LANES // 2, 1)
            else:
                up = pltpu.roll(b, bit * along, 1)
                down = pltpu.roll(a, LANES - bit * along, 1)
            mixed[c] = jnp.where(upper, up, a)
            mixed[c | bit] = jnp.where(upper, b, down)
        parts = mixed
        bit *= 2
    return parts


def swap_rows(parts, sub):
    bit = 1
    while bit < len(parts):
        upper = sub & bit != 0
        mixed = list(parts)
        for c in range(len(parts)):
            if c & bit:
                continue
            a, b = parts[c], parts[c | bit]
            both = jnp.where(upper, a, b)
            mixed[c] = jnp.where(upper, pltpu.roll(both, bit, 0), a)
            mixed[c | bit] = jnp.where(upper, b, pltpu.roll(both, 8 - bit, 0))
        parts = mixed
        bit *= 2
    return parts


def place_kernel(
    in_ref, out_hbm, stage, sem, *, width_x, width_y, rows, message, across, along, scale
):
    devices = width_x * width_y
    halves = across * along // LANES
    chunks = LANES // along
    groups = width_y // chunks
    sums = in_ref[pl.ds(halves * rows, devices, stride=message), :]
    inverse = 1.0 / (jnp.sum(sums) * scale + 1e-06)
    lane = lax.broadcasted_iota(jnp.int32, (1, LANES), 1)
    sub = lax.broadcasted_iota(jnp.int32, (8, 1), 0)
    outer, inner = stage.shape[1:3]
    tiles = width_x * groups
    for tile in range(tiles):
        heads = [(tile * chunks + c) * message for c in range(chunks)]
        for u in range(outer):
            if inner == RADIX:
                spans = [pl.ds(head + u, halves * inner, stride=outer) for head in heads]
                parts = [jnp.log(1.0 + in_ref[span, :] * inverse) for span in spans]
                parts = swap_rows(swap_chunks(parts, along, lane), sub)
                for q in range(inner):
                    stage[tile, u, q] = parts[q]
            else:
                for h in range(halves):
                    spans = [pl.ds(head + h * rows, inner) for head in heads]
                    parts = [jnp.log(1.0 + in_ref[span, :] * inverse) for span in spans]
                    parts = swap_chunks(parts, along, lane)
                    for a in range(chunks):
                        stage[tile, u, :, h * chunks + a, :] = parts[a]
        if tile % BATCH == BATCH - 1:
            for done in range(tile + 1 - BATCH, tile + 1):
                pltpu.make_async_copy(
                    stage.at[done],
                    out_hbm.at[:, :, done // groups, done % groups],
                    sem,
                ).start()
    pltpu.make_async_copy(stage, stage, sem).wait()


def local_call(spectra, resample_index, resample_weight, disp_phase, surface_block, devices):
    across, along, samples = spectra.shape
    count = across * along
    rows = KEEP * BLOCK // devices
    halves = count // LANES
    message = halves * rows + 1
    short = samples // RADIX
    terms = samples // 2 // RADIX
    pieces = samples // LANES
    vmem = pl.BlockSpec(memory_space=pltpu.VMEM)
    hbm = pl.BlockSpec(memory_space=pltpu.HBM)
    return pl.pallas_call(
        functools.partial(local_kernel, devices=devices, rows=rows, message=message),
        out_shape=jax.ShapeDtypeStruct((devices * message, LANES), jnp.float32),
        in_specs=[hbm] * 5,
        out_specs=vmem,
        scratch_shapes=[
            pltpu.VMEM((RADIX, terms, short), jnp.bfloat16),
            pltpu.VMEM((count, samples), jnp.bfloat16),
            pltpu.VMEM((pieces, LANES), jnp.int32),
            pltpu.VMEM((pieces, LANES), jnp.float32),
            pltpu.VMEM((pieces, LANES), jnp.float32),
            pltpu.VMEM((across, along), jnp.int32),
            pltpu.VMEM((pieces, count, LANES), jnp.bfloat16),
            pltpu.VMEM((pieces, count, LANES), jnp.bfloat16),
            pltpu.VMEM((halves, RADIX, 2 * LANES, short), jnp.bfloat16),
            pltpu.VMEM((8, LANES), jnp.float32),
            pltpu.SMEM((2 * pieces,), jnp.int32),
            pltpu.SemaphoreType.DMA((5,)),
        ],
        compiler_params=pltpu.CompilerParams(vmem_limit_bytes=LIMIT),
        name="local",
    )(
        spectra.reshape(count, samples),
        resample_index.reshape(pieces, LANES),
        resample_weight.reshape(pieces, LANES),
        disp_phase.reshape(pieces, LANES),
        surface_block,
    )


def place_call(moved, rows, width_x, width_y, across, along):
    devices = width_x * width_y
    count = across * along
    halves = count // LANES
    message = halves * rows + 1
    height, width = width_x * across, width_y * along
    groups = width // LANES
    vmem = pl.BlockSpec(memory_space=pltpu.VMEM)
    hbm = pl.BlockSpec(memory_space=pltpu.HBM)
    inner = rows if rows % RADIX else RADIX
    placed = pl.pallas_call(
        functools.partial(
            place_kernel,
            width_x=width_x,
            width_y=width_y,
            rows=rows,
            message=message,
            across=across,
            along=along,
            scale=1.0 / (count * KEEP * BLOCK * devices),
        ),
        out_shape=jax.ShapeDtypeStruct(
            (rows // inner, inner, height // 8, groups, 8, LANES), jnp.float32
        ),
        in_specs=[vmem],
        out_specs=hbm,
        scratch_shapes=[
            pltpu.VMEM(
                (width_x * groups, rows // inner, inner, 8, LANES), jnp.float32
            ),
            pltpu.SemaphoreType.DMA,
        ],
        compiler_params=pltpu.CompilerParams(vmem_limit_bytes=8 << 20),
        name="place",
    )(moved)
    placed = placed.reshape(rows, height // 8, groups, 8, LANES)
    return jnp.transpose(placed, (0, 1, 3, 2, 4)).reshape(rows, height, width)


def on_device(spectra, resample_index, resample_weight, disp_phase, surface_block):
    across, along, samples = spectra.shape
    width_x = lax.axis_size("gx")
    width_y = lax.axis_size("gy")
    devices = width_x * width_y
    rows = KEEP * BLOCK // devices
    sent = local_call(
        spectra, resample_index, resample_weight, disp_phase, surface_block, devices
    )
    moved = lax.all_to_all(
        sent.reshape(devices, -1, 1, LANES),
        ("gx", "gy"),
        split_axis=0,
        concat_axis=0,
        tiled=True,
    ).reshape(sent.shape)
    return place_call(moved, rows, width_x, width_y, across, along)


def solution(mesh):
    placed = (P("gx", "gy", None), P(), P(), P(), P("gx", "gy"))
    return jax.shard_map(
        on_device,
        mesh=mesh,
        in_specs=placed,
        out_specs=P(("gx", "gy"), None, None),
        check_vma=False,
    )
```

```python
import functools
import math

import jax
import jax.numpy as jnp
from jax import lax
from jax.experimental import pallas as pl
from jax.experimental.pallas import tpu as pltpu
from jax.sharding import PartitionSpec as P

BLOCK = 128
KEEP = 5
LANES = 128
RADIX = 4
WINDOW = 256
PAIR = 2
BATCH = 4
LIMIT = 24 << 20
COST = 2 << 30
NT = (((1,), (1,)), ((), ()))


def circle(x):
    s = x * x
    cosine = jnp.full_like(x, 1.0 / math.factorial(18))
    sine = jnp.full_like(x, 1.0 / math.factorial(19))
    for k in range(8, -1, -1):
        cosine = 1.0 / math.factorial(2 * k) - s * cosine
        sine = 1.0 / math.factorial(2 * k + 1) - s * sine
    return cosine, sine * x


def unit_circle(turns, samples):
    x = (turns - samples // 2).astype(jnp.float32) * (2.0 * math.pi / samples)
    cosine, sine = circle(x)
    return -cosine, -sine


def place_in_message(r, rows):
    if rows % RADIX:
        return r
    return (r % RADIX) * (rows // RADIX) + r // RADIX


def table_kernel(table, *, samples):
    short = samples // RADIX
    terms = samples // 2 // RADIX
    sub = lax.broadcasted_iota(jnp.int32, (8, short // 2), 0)
    lane = 2 * lax.broadcasted_iota(jnp.int32, (8, short // 2), 1) + 1
    turn = 2 * samples
    bases = [
        unit_circle(((RADIX * sub + q) * lane) & (turn - 1), turn) for q in range(RADIX)
    ]
    for g8 in range(terms // 64):
        rot_c, rot_s = unit_circle((8 * RADIX * (8 * g8 + sub) * lane) & (turn - 1), turn)
        for k in range(0, 8, 2):
            for q in range(RADIX):
                bc, bs = bases[q]
                both = []
                for t in (k, k + 1):
                    rc, rs = rot_c[t : t + 1], rot_s[t : t + 1]
                    both.append((bc * rc - bs * rs, bs * rc + bc * rs))
                row = (8 * g8 + k) * 8
                table[q, row : row + 16, : short // 2] = jnp.concatenate(
                    [both[0][0], both[1][0]], axis=0
                ).astype(jnp.bfloat16)
                table[q, row : row + 16, short // 2 :] = jnp.concatenate(
                    [both[0][1], both[1][1]], axis=0
                ).astype(jnp.bfloat16)


def local_kernel(
    table, spec, idx_in, w_in, phase_in, surf, out_ref,
    idx, weight, phase, real, imag, fold, total, starts,
    *, devices, rows, message,
):
    count, samples = spec.shape
    short = samples // RADIX
    depths = samples // 2
    terms = depths // RADIX
    per_block = BLOCK // RADIX
    blocks = depths // BLOCK
    pieces = samples // LANES
    quarter = pieces // RADIX
    halves = count // LANES

    total[...] = jnp.zeros_like(total)

    piece = lax.broadcasted_iota(jnp.int32, idx.shape, 0)
    back = LANES - 1 - lax.broadcasted_iota(jnp.int32, idx.shape, 1)

    def mirrored(ref):
        v = ref[...]
        turned = jnp.take_along_axis(v, back, axis=1, mode="promise_in_bounds")
        return jnp.where(piece % quarter >= quarter // 2, turned, v)

    index = mirrored(idx_in)
    idx[...] = index
    low = jnp.min(index, axis=1, keepdims=True)
    first = jnp.minimum((low // LANES) * LANES, samples - WINDOW)
    high = jnp.max(index, axis=1, keepdims=True) + 2
    longest = jnp.max(high - first)
    steps = (high - first + (LANES - 1)) // LANES
    phases = mirrored(phase_in)
    phase[...] = phases
    cos_phase, sin_phase = circle(phases)
    ws = mirrored(w_in)
    weight[...] = ws
    vs = 1.0 - ws
    near_all = index - first

    source = lax.broadcasted_iota(jnp.int32, (WINDOW, LANES), 0).astype(jnp.bfloat16)

    def pick(near):
        hits = []
        for k in range(2):
            want = jnp.clip(near + k, -1, WINDOW).astype(jnp.bfloat16)
            hits.append(jnp.where(source == want, jnp.bfloat16(1), jnp.bfloat16(0)))
        return jnp.concatenate(hits, axis=1)

    def finish(pair, v, w, c, s):
        r = v * pair[:, :LANES] + w * pair[:, LANES:]
        return (r * c).astype(jnp.bfloat16), (r * s).astype(jnp.bfloat16)

    for b in range(pieces):
        row = slice(b, b + 1)
        lines = spec[:, pl.ds(pl.multiple_of(first[b, 0], LANES), WINDOW)]
        pair = jnp.dot(lines, pick(near_all[row]), preferred_element_type=jnp.float32)
        real[b], imag[b] = finish(pair, vs[row], ws[row], cos_phase[row], sin_phase[row])

    @pl.when(longest > WINDOW)
    def _():
        for b in range(pieces):
            starts[b] = first[b, 0]
            starts[pieces + b] = steps[b, 0]

        def redo(b, carry):
            @pl.when(starts[pieces + b] * LANES > WINDOW)
            def _():
                near = idx[pl.ds(b, 1), :]

                def step(i, pair):
                    k = pl.multiple_of(starts[b] + i * LANES, LANES)
                    hits = pick(near - k)[:LANES]
                    return pair + jnp.dot(
                        spec[:, pl.ds(k, LANES)],
                        hits,
                        preferred_element_type=jnp.float32,
                    )

                pair = lax.fori_loop(
                    0,
                    starts[pieces + b],
                    step,
                    jnp.zeros((count, 2 * LANES), jnp.float32),
                )
                c, s = circle(phase[pl.ds(b, 1), :])
                w = weight[pl.ds(b, 1), :]
                re, im = finish(pair, 1.0 - w, w, c, s)
                real[b] = re
                imag[b] = im

            return carry

        lax.fori_loop(0, pieces, redo, 0)

    def fold_lines(h, r0):
        at = pl.ds(pl.multiple_of(h * LANES + r0, 16), 16)
        top = pl.ds(pl.multiple_of(r0, 16), 16)
        bottom = pl.ds(pl.multiple_of(LANES + r0, 16), 16)
        for t in range(quarter // 2):
            re, im, re_, im_ = [], [], [], []
            for p in range(RADIX):
                re.append(real[p * quarter + t, at].astype(jnp.float32))
                im.append(imag[p * quarter + t, at].astype(jnp.float32))
                u = (p + 1) * quarter - 1 - t
                re_.append(real[u, at].astype(jnp.float32))
                im_.append(imag[u, at].astype(jnp.float32))
            ar, ai = re[0] + re[2], im[0] + im[2]
            br, bi = re[0] - re[2], im[0] - im[2]
            cr, ci = re[1] + re[3], im[1] + im[3]
            dr, di = re[1] - re[3], im[1] - im[3]
            ar_, ai_ = re_[0] + re_[2], im_[0] + im_[2]
            br_, bi_ = re_[0] - re_[2], im_[0] - im_[2]
            cr_, ci_ = re_[1] + re_[3], im_[1] + im_[3]
            er_, di_ = re_[3] - re_[1], im_[1] - im_[3]
            yz = [
                (ar + cr, ai + ci, ar_ + cr_, ai_ + ci_, True),
                (br + di, bi - dr, bi_ + er_, br_ + di_, False),
                (ar - cr, ai - ci, cr_ - ar_, ci_ - ai_, True),
                (br - di, bi + dr, er_ - bi_, br_ - di_, True),
            ]
            left = slice(t * LANES, (t + 1) * LANES)
            right = slice(short // 2 + t * LANES, short // 2 + (t + 1) * LANES)
            for q, (yr, yi, zr, zi, plus) in enumerate(yz):
                even, odd = (yi + zi, yi - zi) if plus else (yi - zi, yi + zi)
                fold[h, q, top, left] = (yr + zr).astype(jnp.bfloat16)
                fold[h, q, top, right] = odd.astype(jnp.bfloat16)
                fold[h, q, bottom, left] = even.astype(jnp.bfloat16)
                fold[h, q, bottom, right] = (zr - yr).astype(jnp.bfloat16)

    per_half = LANES // surf.shape[1]

    def transform(h, q):
        lines_at = range(h * per_half, (h + 1) * per_half)
        surface = jnp.concatenate([surf[x : x + 1, :] for x in lines_at], axis=1)
        chosen = [surface == s for s in range(1, blocks - KEEP + 1)]
        depth = lax.dot_general(
            table[q], fold[h, q], NT, preferred_element_type=jnp.float32
        )
        re, im = depth[:, :LANES], depth[:, LANES:]
        power = re * re + im * im
        for k in range(KEEP):
            kept = power[k * per_block : (k + 1) * per_block]
            for s, hit in enumerate(chosen, 1):
                there = power[(k + s) * per_block : (k + s + 1) * per_block]
                kept = jnp.where(hit, there, kept)
            total[...] += jnp.sum(kept.reshape(per_block // 8, 8, LANES), axis=0)
            places = []
            for m in range(per_block):
                r = (k * per_block + m) * RADIX + q
                inside = place_in_message(r % rows, rows)
                places.append((r // rows) * message + h * rows + inside)
            m = 0
            while m < per_block:
                stop = m + 1
                while stop % 8 and places[stop] == places[stop - 1] + 1:
                    stop += 1
                out_ref[places[m] : places[m] + stop - m, :] = kept[m:stop]
                m = stop

    @pl.loop(0, LANES // 32)
    def _(chunk):
        for part in range(2):
            fold_lines(0, chunk * 32 + part * 16)

    for h in range(halves):
        for q0 in range(0, RADIX, PAIR):

            @pl.when(longest > 0)
            def _():
                for q in range(q0, q0 + PAIR):
                    transform(h, q)
                if h + 1 < halves:
                    share = LANES * PAIR // RADIX
                    begin = q0 // PAIR * share
                    for r0 in range(begin, begin + share, 16):
                        fold_lines(h + 1, r0)

    partial = jnp.sum(total[...], axis=0, keepdims=True)
    for dest in range(devices):
        at = dest * message + halves * rows
        out_ref[at : at + 1, :] = partial


def swap_chunks(parts, along, lane):
    chunks = len(parts)
    bit = 1
    while bit < chunks:
        upper = (lane // along) & bit != 0
        mixed = list(parts)
        for c in range(chunks):
            if c & bit:
                continue
            a, b = parts[c], parts[c | bit]
            if 2 * bit == chunks:
                up = down = pltpu.roll(jnp.where(upper, a, b), LANES // 2, 1)
            else:
                up = pltpu.roll(b, bit * along, 1)
                down = pltpu.roll(a, LANES - bit * along, 1)
            mixed[c] = jnp.where(upper, up, a)
            mixed[c | bit] = jnp.where(upper, b, down)
        parts = mixed
        bit *= 2
    return parts


def swap_rows(parts, sub):
    bit = 1
    while bit < len(parts):
        upper = sub & bit != 0
        mixed = list(parts)
        for c in range(len(parts)):
            if c & bit:
                continue
            a, b = parts[c], parts[c | bit]
            both = jnp.where(upper, a, b)
            mixed[c] = jnp.where(upper, pltpu.roll(both, bit, 0), a)
            mixed[c | bit] = jnp.where(upper, b, pltpu.roll(both, 8 - bit, 0))
        parts = mixed
        bit *= 2
    return parts


def place_kernel(
    in_ref, out_hbm, stage, sem, *, width_x, width_y, rows, message, across, along, scale
):
    devices = width_x * width_y
    halves = across * along // LANES
    chunks = LANES // along
    groups = width_y // chunks
    sums = in_ref[pl.ds(halves * rows, devices, stride=message), :]
    inverse = 1.0 / (jnp.sum(sums) * scale + 1e-06)
    lane = lax.broadcasted_iota(jnp.int32, (1, LANES), 1)
    sub = lax.broadcasted_iota(jnp.int32, (8, 1), 0)
    outer, inner = stage.shape[1:3]
    tiles = width_x * groups
    for tile in range(tiles):
        heads = [(tile * chunks + c) * message for c in range(chunks)]
        for u in range(outer):
            if inner == RADIX:
                spans = [pl.ds(head + u, halves * inner, stride=outer) for head in heads]
                parts = [jnp.log(1.0 + in_ref[span, :] * inverse) for span in spans]
                parts = swap_rows(swap_chunks(parts, along, lane), sub)
                for q in range(inner):
                    stage[tile, u, q] = parts[q]
            else:
                for h in range(halves):
                    spans = [pl.ds(head + h * rows, inner) for head in heads]
                    parts = [jnp.log(1.0 + in_ref[span, :] * inverse) for span in spans]
                    parts = swap_chunks(parts, along, lane)
                    for a in range(chunks):
                        stage[tile, u, :, h * chunks + a, :] = parts[a]
        if tile % BATCH == BATCH - 1:
            for done in range(tile + 1 - BATCH, tile + 1):
                pltpu.make_async_copy(
                    stage.at[done],
                    out_hbm.at[:, :, done // groups, done % groups],
                    sem,
                ).start()
    pltpu.make_async_copy(stage, stage, sem).wait()


def local_call(spectra, resample_index, resample_weight, disp_phase, surface_block, devices):
    across, along, samples = spectra.shape
    count = across * along
    rows = KEEP * BLOCK // devices
    halves = count // LANES
    message = halves * rows + 1
    short = samples // RADIX
    terms = samples // 2 // RADIX
    pieces = samples // LANES
    vmem = pl.BlockSpec(memory_space=pltpu.VMEM)
    table = pl.pallas_call(
        functools.partial(table_kernel, samples=samples),
        out_shape=jax.ShapeDtypeStruct((RADIX, terms, short), jnp.bfloat16),
        out_specs=vmem,
        cost_estimate=pl.CostEstimate(
            flops=COST, transcendentals=0, bytes_accessed=2 * RADIX * terms * short
        ),
        compiler_params=pltpu.CompilerParams(vmem_limit_bytes=8 << 20),
        name="table",
    )()
    return pl.pallas_call(
        functools.partial(local_kernel, devices=devices, rows=rows, message=message),
        out_shape=jax.ShapeDtypeStruct((devices * message, LANES), jnp.float32),
        in_specs=[vmem] * 6,
        out_specs=vmem,
        scratch_shapes=[
            pltpu.VMEM((pieces, LANES), jnp.int32),
            pltpu.VMEM((pieces, LANES), jnp.float32),
            pltpu.VMEM((pieces, LANES), jnp.float32),
            pltpu.VMEM((pieces, count, LANES), jnp.bfloat16),
            pltpu.VMEM((pieces, count, LANES), jnp.bfloat16),
            pltpu.VMEM((halves, RADIX, 2 * LANES, short), jnp.bfloat16),
            pltpu.VMEM((8, LANES), jnp.float32),
            pltpu.SMEM((2 * pieces,), jnp.int32),
        ],
        compiler_params=pltpu.CompilerParams(vmem_limit_bytes=LIMIT),
        name="local",
    )(
        table,
        spectra.reshape(count, samples),
        resample_index.reshape(pieces, LANES),
        resample_weight.reshape(pieces, LANES),
        disp_phase.reshape(pieces, LANES),
        surface_block,
    )


def place_call(moved, rows, width_x, width_y, across, along):
    devices = width_x * width_y
    count = across * along
    halves = count // LANES
    message = halves * rows + 1
    height, width = width_x * across, width_y * along
    groups = width // LANES
    vmem = pl.BlockSpec(memory_space=pltpu.VMEM)
    hbm = pl.BlockSpec(memory_space=pltpu.HBM)
    inner = rows if rows % RADIX else RADIX
    placed = pl.pallas_call(
        functools.partial(
            place_kernel,
            width_x=width_x,
            width_y=width_y,
            rows=rows,
            message=message,
            across=across,
            along=along,
            scale=1.0 / (count * KEEP * BLOCK * devices),
        ),
        out_shape=jax.ShapeDtypeStruct(
            (rows // inner, inner, height // 8, groups, 8, LANES), jnp.float32
        ),
        in_specs=[vmem],
        out_specs=hbm,
        scratch_shapes=[
            pltpu.VMEM(
                (width_x * groups, rows // inner, inner, 8, LANES), jnp.float32
            ),
            pltpu.SemaphoreType.DMA,
        ],
        compiler_params=pltpu.CompilerParams(vmem_limit_bytes=8 << 20),
        name="place",
    )(moved)
    placed = placed.reshape(rows, height // 8, groups, 8, LANES)
    return jnp.transpose(placed, (0, 1, 3, 2, 4)).reshape(rows, height, width)


def on_device(spectra, resample_index, resample_weight, disp_phase, surface_block):
    across, along, samples = spectra.shape
    width_x = lax.axis_size("gx")
    width_y = lax.axis_size("gy")
    devices = width_x * width_y
    rows = KEEP * BLOCK // devices
    sent = local_call(
        spectra, resample_index, resample_weight, disp_phase, surface_block, devices
    )
    moved = lax.all_to_all(
        sent.reshape(devices, -1, 1, LANES),
        ("gx", "gy"),
        split_axis=0,
        concat_axis=0,
        tiled=True,
    ).reshape(sent.shape)
    return place_call(moved, rows, width_x, width_y, across, along)


def solution(mesh):
    placed = (P("gx", "gy", None), P(), P(), P(), P("gx", "gy"))
    return jax.shard_map(
        on_device,
        mesh=mesh,
        in_specs=placed,
        out_specs=P(("gx", "gy"), None, None),
        check_vma=False,
    )
```

```python
import functools
import math

import jax
import jax.numpy as jnp
from jax import lax
from jax.experimental import pallas as pl
from jax.experimental.pallas import tpu as pltpu
from jax.sharding import PartitionSpec as P

BLOCK = 128
KEEP = 5
LANES = 128
RADIX = 4
WINDOW = 256
PAIR = 2
BATCH = 4
LIMIT = 24 << 20
COST = 2 << 30
NT = (((1,), (1,)), ((), ()))


def circle(x):
    s = x * x
    cosine = jnp.full_like(x, 1.0 / math.factorial(18))
    sine = jnp.full_like(x, 1.0 / math.factorial(19))
    for k in range(8, -1, -1):
        cosine = 1.0 / math.factorial(2 * k) - s * cosine
        sine = 1.0 / math.factorial(2 * k + 1) - s * sine
    return cosine, sine * x


def unit_circle(turns, samples):
    x = (turns - samples // 2).astype(jnp.float32) * (2.0 * math.pi / samples)
    cosine, sine = circle(x)
    return -cosine, -sine


def place_in_message(r, rows):
    if rows % RADIX:
        return r
    return (r % RADIX) * (rows // RADIX) + r // RADIX


def table_kernel(table, *, samples):
    short = samples // RADIX
    terms = samples // 2 // RADIX
    sub = lax.broadcasted_iota(jnp.int32, (8, short // 2), 0)
    lane = 2 * lax.broadcasted_iota(jnp.int32, (8, short // 2), 1) + 1
    turn = 2 * samples
    bases = [
        unit_circle(((RADIX * sub + q) * lane) & (turn - 1), turn) for q in range(RADIX)
    ]
    for g8 in range(terms // 64):
        rot_c, rot_s = unit_circle((8 * RADIX * (8 * g8 + sub) * lane) & (turn - 1), turn)
        for k in range(0, 8, 2):
            for q in range(RADIX):
                bc, bs = bases[q]
                both = []
                for t in (k, k + 1):
                    rc, rs = rot_c[t : t + 1], rot_s[t : t + 1]
                    both.append((bc * rc - bs * rs, bs * rc + bc * rs))
                row = (8 * g8 + k) * 8
                table[q, row : row + 16, : short // 2] = jnp.concatenate(
                    [both[0][0], both[1][0]], axis=0
                ).astype(jnp.bfloat16)
                table[q, row : row + 16, short // 2 :] = jnp.concatenate(
                    [both[0][1], both[1][1]], axis=0
                ).astype(jnp.bfloat16)


def pick(near):
    source = lax.broadcasted_iota(jnp.int32, (WINDOW, LANES), 0).astype(jnp.bfloat16)
    hits = []
    for k in range(2):
        want = jnp.clip(near + k, -1, WINDOW).astype(jnp.bfloat16)
        hits.append(jnp.where(source == want, jnp.bfloat16(1), jnp.bfloat16(0)))
    return jnp.concatenate(hits, axis=1)


def finish(pair, w, c, s):
    r = (1.0 - w) * pair[:, :LANES] + w * pair[:, LANES:]
    return (r * c).astype(jnp.bfloat16), (r * s).astype(jnp.bfloat16)


def plan_kernel(
    idx_in, w_in, phase_in, picks, idx, weight, cosine, sine, first, spans, *, samples
):
    pieces = samples // LANES
    quarter = pieces // RADIX
    piece = lax.broadcasted_iota(jnp.int32, idx.shape, 0)
    back = LANES - 1 - lax.broadcasted_iota(jnp.int32, idx.shape, 1)

    def mirrored(ref):
        v = ref[...]
        turned = jnp.take_along_axis(v, back, axis=1, mode="promise_in_bounds")
        return jnp.where(piece % quarter >= quarter // 2, turned, v)

    index = mirrored(idx_in)
    idx[...] = index
    low = jnp.min(index, axis=1, keepdims=True)
    start = jnp.minimum((low // LANES) * LANES, samples - WINDOW)
    first[...] = jnp.broadcast_to(start, first.shape)
    spans[...] = jnp.broadcast_to(
        jnp.max(index, axis=1, keepdims=True) + 2 - start, spans.shape
    )
    weight[...] = mirrored(w_in)
    cosine[...], sine[...] = circle(mirrored(phase_in))
    for b in range(pieces):
        picks[b] = pick(index[b : b + 1] - start[b : b + 1])


def local_kernel(
    table, spec, picks, idx, weight, cosine, sine, first, spans, surf, out_ref,
    real, imag, fold, total, starts,
    *, devices, rows, message,
):
    count, samples = spec.shape
    short = samples // RADIX
    depths = samples // 2
    terms = depths // RADIX
    per_block = BLOCK // RADIX
    blocks = depths // BLOCK
    pieces = samples // LANES
    quarter = pieces // RADIX
    halves = count // LANES

    total[...] = jnp.zeros_like(total)

    longest = jnp.max(spans[...])
    for b in range(pieces):
        row = pl.ds(b, 1)
        lines = spec[:, pl.ds(pl.multiple_of(first[b, 0], LANES), WINDOW)]
        pair = jnp.dot(lines, picks[b], preferred_element_type=jnp.float32)
        real[b], imag[b] = finish(pair, weight[row], cosine[row], sine[row])

    @pl.when(longest > WINDOW)
    def _():
        for b in range(pieces):
            starts[b] = first[b, 0]
            starts[pieces + b] = (spans[b, 0] + (LANES - 1)) // LANES

        def redo(b, carry):
            @pl.when(starts[pieces + b] * LANES > WINDOW)
            def _():
                near = idx[pl.ds(b, 1), :]

                def step(i, pair):
                    k = pl.multiple_of(starts[b] + i * LANES, LANES)
                    hits = pick(near - k)[:LANES]
                    return pair + jnp.dot(
                        spec[:, pl.ds(k, LANES)],
                        hits,
                        preferred_element_type=jnp.float32,
                    )

                pair = lax.fori_loop(
                    0,
                    starts[pieces + b],
                    step,
                    jnp.zeros((count, 2 * LANES), jnp.float32),
                )
                row = pl.ds(b, 1)
                re, im = finish(pair, weight[row], cosine[row], sine[row])
                real[b] = re
                imag[b] = im

            return carry

        lax.fori_loop(0, pieces, redo, 0)

    def fold_lines(h, r0):
        at = pl.ds(pl.multiple_of(h * LANES + r0, 16), 16)
        top = pl.ds(pl.multiple_of(r0, 16), 16)
        bottom = pl.ds(pl.multiple_of(LANES + r0, 16), 16)
        for t in range(quarter // 2):
            re, im, re_, im_ = [], [], [], []
            for p in range(RADIX):
                re.append(real[p * quarter + t, at].astype(jnp.float32))
                im.append(imag[p * quarter + t, at].astype(jnp.float32))
                u = (p + 1) * quarter - 1 - t
                re_.append(real[u, at].astype(jnp.float32))
                im_.append(imag[u, at].astype(jnp.float32))
            ar, ai = re[0] + re[2], im[0] + im[2]
            br, bi = re[0] - re[2], im[0] - im[2]
            cr, ci = re[1] + re[3], im[1] + im[3]
            dr, di = re[1] - re[3], im[1] - im[3]
            ar_, ai_ = re_[0] + re_[2], im_[0] + im_[2]
            br_, bi_ = re_[0] - re_[2], im_[0] - im_[2]
            cr_, ci_ = re_[1] + re_[3], im_[1] + im_[3]
            er_, di_ = re_[3] - re_[1], im_[1] - im_[3]
            yz = [
                (ar + cr, ai + ci, ar_ + cr_, ai_ + ci_, True),
                (br + di, bi - dr, bi_ + er_, br_ + di_, False),
                (ar - cr, ai - ci, cr_ - ar_, ci_ - ai_, True),
                (br - di, bi + dr, er_ - bi_, br_ - di_, True),
            ]
            left = slice(t * LANES, (t + 1) * LANES)
            right = slice(short // 2 + t * LANES, short // 2 + (t + 1) * LANES)
            for q, (yr, yi, zr, zi, plus) in enumerate(yz):
                even, odd = (yi + zi, yi - zi) if plus else (yi - zi, yi + zi)
                fold[h, q, top, left] = (yr + zr).astype(jnp.bfloat16)
                fold[h, q, top, right] = odd.astype(jnp.bfloat16)
                fold[h, q, bottom, left] = even.astype(jnp.bfloat16)
                fold[h, q, bottom, right] = (zr - yr).astype(jnp.bfloat16)

    per_half = LANES // surf.shape[1]

    def transform(h, q):
        lines_at = range(h * per_half, (h + 1) * per_half)
        surface = jnp.concatenate([surf[x : x + 1, :] for x in lines_at], axis=1)
        chosen = [surface == s for s in range(1, blocks - KEEP + 1)]
        depth = lax.dot_general(
            table[q], fold[h, q], NT, preferred_element_type=jnp.float32
        )
        re, im = depth[:, :LANES], depth[:, LANES:]
        power = re * re + im * im
        for k in range(KEEP):
            kept = power[k * per_block : (k + 1) * per_block]
            for s, hit in enumerate(chosen, 1):
                there = power[(k + s) * per_block : (k + s + 1) * per_block]
                kept = jnp.where(hit, there, kept)
            total[...] += jnp.sum(kept.reshape(per_block // 8, 8, LANES), axis=0)
            places = []
            for m in range(per_block):
                r = (k * per_block + m) * RADIX + q
                inside = place_in_message(r % rows, rows)
                places.append((r // rows) * message + h * rows + inside)
            m = 0
            while m < per_block:
                stop = m + 1
                while stop % 8 and places[stop] == places[stop - 1] + 1:
                    stop += 1
                out_ref[places[m] : places[m] + stop - m, :] = kept[m:stop]
                m = stop

    @pl.loop(0, LANES // 32)
    def _(chunk):
        for part in range(2):
            fold_lines(0, chunk * 32 + part * 16)

    for h in range(halves):
        for q0 in range(0, RADIX, PAIR):

            @pl.when(longest > 0)
            def _():
                for q in range(q0, q0 + PAIR):
                    transform(h, q)
                if h + 1 < halves:
                    share = LANES * PAIR // RADIX
                    begin = q0 // PAIR * share
                    for r0 in range(begin, begin + share, 16):
                        fold_lines(h + 1, r0)

    partial = jnp.sum(total[...], axis=0, keepdims=True)
    for dest in range(devices):
        at = dest * message + halves * rows
        out_ref[at : at + 1, :] = partial


def swap_chunks(parts, along, lane):
    chunks = len(parts)
    bit = 1
    while bit < chunks:
        upper = (lane // along) & bit != 0
        mixed = list(parts)
        for c in range(chunks):
            if c & bit:
                continue
            a, b = parts[c], parts[c | bit]
            if 2 * bit == chunks:
                up = down = pltpu.roll(jnp.where(upper, a, b), LANES // 2, 1)
            else:
                up = pltpu.roll(b, bit * along, 1)
                down = pltpu.roll(a, LANES - bit * along, 1)
            mixed[c] = jnp.where(upper, up, a)
            mixed[c | bit] = jnp.where(upper, b, down)
        parts = mixed
        bit *= 2
    return parts


def swap_rows(parts, sub):
    bit = 1
    while bit < len(parts):
        upper = sub & bit != 0
        mixed = list(parts)
        for c in range(len(parts)):
            if c & bit:
                continue
            a, b = parts[c], parts[c | bit]
            both = jnp.where(upper, a, b)
            mixed[c] = jnp.where(upper, pltpu.roll(both, bit, 0), a)
            mixed[c | bit] = jnp.where(upper, b, pltpu.roll(both, 8 - bit, 0))
        parts = mixed
        bit *= 2
    return parts


def place_kernel(
    in_ref, out_hbm, stage, sem, *, width_x, width_y, rows, message, across, along, scale
):
    devices = width_x * width_y
    halves = across * along // LANES
    chunks = LANES // along
    groups = width_y // chunks
    sums = in_ref[pl.ds(halves * rows, devices, stride=message), :]
    inverse = 1.0 / (jnp.sum(sums) * scale + 1e-06)
    lane = lax.broadcasted_iota(jnp.int32, (1, LANES), 1)
    sub = lax.broadcasted_iota(jnp.int32, (8, 1), 0)
    outer, inner = stage.shape[1:3]
    tiles = width_x * groups
    for tile in range(tiles):
        heads = [(tile * chunks + c) * message for c in range(chunks)]
        for u in range(outer):
            if inner == RADIX:
                spans = [pl.ds(head + u, halves * inner, stride=outer) for head in heads]
                parts = [jnp.log(1.0 + in_ref[span, :] * inverse) for span in spans]
                parts = swap_rows(swap_chunks(parts, along, lane), sub)
                for q in range(inner):
                    stage[tile, u, q] = parts[q]
            else:
                for h in range(halves):
                    spans = [pl.ds(head + h * rows, inner) for head in heads]
                    parts = [jnp.log(1.0 + in_ref[span, :] * inverse) for span in spans]
                    parts = swap_chunks(parts, along, lane)
                    for a in range(chunks):
                        stage[tile, u, :, h * chunks + a, :] = parts[a]
        if tile % BATCH == BATCH - 1:
            for done in range(tile + 1 - BATCH, tile + 1):
                pltpu.make_async_copy(
                    stage.at[done],
                    out_hbm.at[:, :, done // groups, done % groups],
                    sem,
                ).start()
    pltpu.make_async_copy(stage, stage, sem).wait()


def local_call(spectra, resample_index, resample_weight, disp_phase, surface_block, devices):
    across, along, samples = spectra.shape
    count = across * along
    rows = KEEP * BLOCK // devices
    halves = count // LANES
    message = halves * rows + 1
    short = samples // RADIX
    terms = samples // 2 // RADIX
    pieces = samples // LANES
    vmem = pl.BlockSpec(memory_space=pltpu.VMEM)
    table = pl.pallas_call(
        functools.partial(table_kernel, samples=samples),
        out_shape=jax.ShapeDtypeStruct((RADIX, terms, short), jnp.bfloat16),
        out_specs=vmem,
        cost_estimate=pl.CostEstimate(
            flops=COST, transcendentals=0, bytes_accessed=2 * RADIX * terms * short
        ),
        compiler_params=pltpu.CompilerParams(vmem_limit_bytes=8 << 20),
        name="table",
    )()
    line = lambda dtype: jax.ShapeDtypeStruct((pieces, LANES), dtype)
    plan = pl.pallas_call(
        functools.partial(plan_kernel, samples=samples),
        out_shape=(
            jax.ShapeDtypeStruct((pieces, WINDOW, 2 * LANES), jnp.bfloat16),
            line(jnp.int32),
            line(jnp.float32),
            line(jnp.float32),
            line(jnp.float32),
            line(jnp.int32),
            line(jnp.int32),
        ),
        in_specs=[vmem] * 3,
        out_specs=(vmem,) * 7,
        cost_estimate=pl.CostEstimate(
            flops=1, transcendentals=0, bytes_accessed=1
        ),
        compiler_params=pltpu.CompilerParams(vmem_limit_bytes=8 << 20),
        name="plan",
    )(
        resample_index.reshape(pieces, LANES),
        resample_weight.reshape(pieces, LANES),
        disp_phase.reshape(pieces, LANES),
    )
    return pl.pallas_call(
        functools.partial(local_kernel, devices=devices, rows=rows, message=message),
        out_shape=jax.ShapeDtypeStruct((devices * message, LANES), jnp.float32),
        in_specs=[vmem] * 10,
        out_specs=vmem,
        scratch_shapes=[
            pltpu.VMEM((pieces, count, LANES), jnp.bfloat16),
            pltpu.VMEM((pieces, count, LANES), jnp.bfloat16),
            pltpu.VMEM((halves, RADIX, 2 * LANES, short), jnp.bfloat16),
            pltpu.VMEM((8, LANES), jnp.float32),
            pltpu.SMEM((2 * pieces,), jnp.int32),
        ],
        compiler_params=pltpu.CompilerParams(vmem_limit_bytes=LIMIT),
        name="local",
    )(table, spectra.reshape(count, samples), *plan, surface_block)


def place_call(moved, rows, width_x, width_y, across, along):
    devices = width_x * width_y
    count = across * along
    halves = count // LANES
    message = halves * rows + 1
    height, width = width_x * across, width_y * along
    groups = width // LANES
    vmem = pl.BlockSpec(memory_space=pltpu.VMEM)
    hbm = pl.BlockSpec(memory_space=pltpu.HBM)
    inner = rows if rows % RADIX else RADIX
    placed = pl.pallas_call(
        functools.partial(
            place_kernel,
            width_x=width_x,
            width_y=width_y,
            rows=rows,
            message=message,
            across=across,
            along=along,
            scale=1.0 / (count * KEEP * BLOCK * devices),
        ),
        out_shape=jax.ShapeDtypeStruct(
            (rows // inner, inner, height // 8, groups, 8, LANES), jnp.float32
        ),
        in_specs=[vmem],
        out_specs=hbm,
        scratch_shapes=[
            pltpu.VMEM(
                (width_x * groups, rows // inner, inner, 8, LANES), jnp.float32
            ),
            pltpu.SemaphoreType.DMA,
        ],
        compiler_params=pltpu.CompilerParams(vmem_limit_bytes=8 << 20),
        name="place",
    )(moved)
    placed = placed.reshape(rows, height // 8, groups, 8, LANES)
    return jnp.transpose(placed, (0, 1, 3, 2, 4)).reshape(rows, height, width)


def on_device(spectra, resample_index, resample_weight, disp_phase, surface_block):
    across, along, samples = spectra.shape
    width_x = lax.axis_size("gx")
    width_y = lax.axis_size("gy")
    devices = width_x * width_y
    rows = KEEP * BLOCK // devices
    sent = local_call(
        spectra, resample_index, resample_weight, disp_phase, surface_block, devices
    )
    moved = lax.all_to_all(
        sent.reshape(devices, -1, 1, LANES),
        ("gx", "gy"),
        split_axis=0,
        concat_axis=0,
        tiled=True,
    ).reshape(sent.shape)
    return place_call(moved, rows, width_x, width_y, across, along)


def solution(mesh):
    placed = (P("gx", "gy", None), P(), P(), P(), P("gx", "gy"))
    return jax.shard_map(
        on_device,
        mesh=mesh,
        in_specs=placed,
        out_specs=P(("gx", "gy"), None, None),
        check_vma=False,
    )
```

```python
import functools
import math

import jax
import jax.numpy as jnp
from jax import lax
from jax.experimental import pallas as pl
from jax.experimental.pallas import tpu as pltpu
from jax.sharding import PartitionSpec as P

BLOCK = 128
KEEP = 5
LANES = 128
RADIX = 4
WINDOW = 256
PAIR = 2
BATCH = 4
LIMIT = 24 << 20
COST = 2 << 30
NT = (((1,), (1,)), ((), ()))


def circle(x):
    s = x * x
    cosine = jnp.full_like(x, 1.0 / math.factorial(18))
    sine = jnp.full_like(x, 1.0 / math.factorial(19))
    for k in range(8, -1, -1):
        cosine = 1.0 / math.factorial(2 * k) - s * cosine
        sine = 1.0 / math.factorial(2 * k + 1) - s * sine
    return cosine, sine * x


def unit_circle(turns, samples):
    x = (turns - samples // 2).astype(jnp.float32) * (2.0 * math.pi / samples)
    cosine, sine = circle(x)
    return -cosine, -sine


def place_in_message(r, rows):
    if rows % RADIX:
        return r
    return (r % RADIX) * (rows // RADIX) + r // RADIX


def make_table(table, samples):
    short = samples // RADIX
    terms = samples // 2 // RADIX
    sub = lax.broadcasted_iota(jnp.int32, (8, short // 2), 0)
    lane = 2 * lax.broadcasted_iota(jnp.int32, (8, short // 2), 1) + 1
    turn = 2 * samples
    bases = [
        unit_circle(((RADIX * sub + q) * lane) & (turn - 1), turn) for q in range(RADIX)
    ]
    for g8 in range(terms // 64):
        rot_c, rot_s = unit_circle((8 * RADIX * (8 * g8 + sub) * lane) & (turn - 1), turn)
        for k in range(0, 8, 2):
            for q in range(RADIX):
                bc, bs = bases[q]
                both = []
                for t in (k, k + 1):
                    rc, rs = rot_c[t : t + 1], rot_s[t : t + 1]
                    both.append((bc * rc - bs * rs, bs * rc + bc * rs))
                row = (8 * g8 + k) * 8
                table[q, row : row + 16, : short // 2] = jnp.concatenate(
                    [both[0][0], both[1][0]], axis=0
                ).astype(jnp.bfloat16)
                table[q, row : row + 16, short // 2 :] = jnp.concatenate(
                    [both[0][1], both[1][1]], axis=0
                ).astype(jnp.bfloat16)


def pick(near):
    source = lax.broadcasted_iota(jnp.int32, (WINDOW, LANES), 0).astype(jnp.bfloat16)
    hits = []
    for k in range(2):
        want = jnp.clip(near + k, -1, WINDOW).astype(jnp.bfloat16)
        hits.append(jnp.where(source == want, jnp.bfloat16(1), jnp.bfloat16(0)))
    return jnp.concatenate(hits, axis=1)


def finish(pair, w, c, s):
    r = (1.0 - w) * pair[:, :LANES] + w * pair[:, LANES:]
    rounded = lambda v: v.astype(jnp.bfloat16).astype(jnp.float32)
    return rounded(r * c), rounded(r * s)


def plan_kernel(
    idx_hbm, w_hbm, phase_hbm, table, picks, idx, weight, cosine, sine, first, spans,
    idx_in, w_in, phase_in, sems, *, samples,
):
    pairs = ((idx_hbm, idx_in), (w_hbm, w_in), (phase_hbm, phase_in))
    copies = [
        pltpu.make_async_copy(a, b, sems.at[i]) for i, (a, b) in enumerate(pairs)
    ]
    for copy in copies:
        copy.start()
    make_table(table, samples)
    for copy in copies:
        copy.wait()
    pieces = samples // LANES
    quarter = pieces // RADIX
    piece = lax.broadcasted_iota(jnp.int32, idx.shape, 0)
    back = LANES - 1 - lax.broadcasted_iota(jnp.int32, idx.shape, 1)

    def mirrored(ref):
        v = ref[...]
        turned = jnp.take_along_axis(v, back, axis=1, mode="promise_in_bounds")
        return jnp.where(piece % quarter >= quarter // 2, turned, v)

    index = mirrored(idx_in)
    idx[...] = index
    low = jnp.min(index, axis=1, keepdims=True)
    start = jnp.minimum((low // LANES) * LANES, samples - WINDOW)
    first[...] = jnp.broadcast_to(start, first.shape)
    spans[...] = jnp.broadcast_to(
        jnp.max(index, axis=1, keepdims=True) + 2 - start, spans.shape
    )
    weight[...] = mirrored(w_in)
    cosine[...], sine[...] = circle(mirrored(phase_in))
    for b in range(pieces):
        picks[b] = pick(index[b : b + 1] - start[b : b + 1])


def local_kernel(
    table, spec, picks, idx, weight, cosine, sine, first, spans, surf, out_ref,
    real, imag, fold, total, starts,
    *, devices, rows, message,
):
    count, samples = spec.shape
    short = samples // RADIX
    depths = samples // 2
    terms = depths // RADIX
    per_block = BLOCK // RADIX
    blocks = depths // BLOCK
    pieces = samples // LANES
    quarter = pieces // RADIX
    halves = count // LANES

    total[...] = jnp.zeros_like(total)

    longest = jnp.max(spans[...])
    for b in range(pieces):
        row = pl.ds(b, 1)
        lines = spec[:, pl.ds(pl.multiple_of(first[b, 0], LANES), WINDOW)]
        pair = jnp.dot(lines, picks[b], preferred_element_type=jnp.float32)
        real[b], imag[b] = finish(pair, weight[row], cosine[row], sine[row])

    @pl.when(longest > WINDOW)
    def _():
        for b in range(pieces):
            starts[b] = first[b, 0]
            starts[pieces + b] = (spans[b, 0] + (LANES - 1)) // LANES

        def redo(b, carry):
            @pl.when(starts[pieces + b] * LANES > WINDOW)
            def _():
                near = idx[pl.ds(b, 1), :]

                def step(i, pair):
                    k = pl.multiple_of(starts[b] + i * LANES, LANES)
                    hits = pick(near - k)[:LANES]
                    return pair + jnp.dot(
                        spec[:, pl.ds(k, LANES)],
                        hits,
                        preferred_element_type=jnp.float32,
                    )

                pair = lax.fori_loop(
                    0,
                    starts[pieces + b],
                    step,
                    jnp.zeros((count, 2 * LANES), jnp.float32),
                )
                row = pl.ds(b, 1)
                re, im = finish(pair, weight[row], cosine[row], sine[row])
                real[b] = re
                imag[b] = im

            return carry

        lax.fori_loop(0, pieces, redo, 0)

    def fold_lines(h, r0):
        at = pl.ds(pl.multiple_of(h * LANES + r0, 16), 16)
        top = pl.ds(pl.multiple_of(r0, 16), 16)
        bottom = pl.ds(pl.multiple_of(LANES + r0, 16), 16)
        for t in range(quarter // 2):
            re, im, re_, im_ = [], [], [], []
            for p in range(RADIX):
                re.append(real[p * quarter + t, at])
                im.append(imag[p * quarter + t, at])
                u = (p + 1) * quarter - 1 - t
                re_.append(real[u, at])
                im_.append(imag[u, at])
            ar, ai = re[0] + re[2], im[0] + im[2]
            br, bi = re[0] - re[2], im[0] - im[2]
            cr, ci = re[1] + re[3], im[1] + im[3]
            dr, di = re[1] - re[3], im[1] - im[3]
            ar_, ai_ = re_[0] + re_[2], im_[0] + im_[2]
            br_, bi_ = re_[0] - re_[2], im_[0] - im_[2]
            cr_, ci_ = re_[1] + re_[3], im_[1] + im_[3]
            er_, di_ = re_[3] - re_[1], im_[1] - im_[3]
            yz = [
                (ar + cr, ai + ci, ar_ + cr_, ai_ + ci_, True),
                (br + di, bi - dr, bi_ + er_, br_ + di_, False),
                (ar - cr, ai - ci, cr_ - ar_, ci_ - ai_, True),
                (br - di, bi + dr, er_ - bi_, br_ - di_, True),
            ]
            left = slice(t * LANES, (t + 1) * LANES)
            right = slice(short // 2 + t * LANES, short // 2 + (t + 1) * LANES)
            for q, (yr, yi, zr, zi, plus) in enumerate(yz):
                even, odd = (yi + zi, yi - zi) if plus else (yi - zi, yi + zi)
                fold[h, q, top, left] = (yr + zr).astype(jnp.bfloat16)
                fold[h, q, top, right] = odd.astype(jnp.bfloat16)
                fold[h, q, bottom, left] = even.astype(jnp.bfloat16)
                fold[h, q, bottom, right] = (zr - yr).astype(jnp.bfloat16)

    per_half = LANES // surf.shape[1]

    def transform(h, q):
        lines_at = range(h * per_half, (h + 1) * per_half)
        surface = jnp.concatenate([surf[x : x + 1, :] for x in lines_at], axis=1)
        chosen = [surface == s for s in range(1, blocks - KEEP + 1)]
        depth = lax.dot_general(
            table[q], fold[h, q], NT, preferred_element_type=jnp.float32
        )
        re, im = depth[:, :LANES], depth[:, LANES:]
        power = re * re + im * im
        for k in range(KEEP):
            kept = power[k * per_block : (k + 1) * per_block]
            for s, hit in enumerate(chosen, 1):
                there = power[(k + s) * per_block : (k + s + 1) * per_block]
                kept = jnp.where(hit, there, kept)
            total[...] += jnp.sum(kept.reshape(per_block // 8, 8, LANES), axis=0)
            places = []
            for m in range(per_block):
                r = (k * per_block + m) * RADIX + q
                inside = place_in_message(r % rows, rows)
                places.append((r // rows) * message + h * rows + inside)
            m = 0
            while m < per_block:
                stop = m + 1
                while stop % 8 and places[stop] == places[stop - 1] + 1:
                    stop += 1
                out_ref[places[m] : places[m] + stop - m, :] = kept[m:stop]
                m = stop

    for h in range(halves):
        for r0 in range(0, LANES, 16):
            fold_lines(h, r0)

    for h in range(halves):
        for q in range(RADIX):
            transform(h, q)

    partial = jnp.sum(total[...], axis=0, keepdims=True)
    for dest in range(devices):
        at = dest * message + halves * rows
        out_ref[at : at + 1, :] = partial


def swap_chunks(parts, along, lane):
    chunks = len(parts)
    bit = 1
    while bit < chunks:
        upper = (lane // along) & bit != 0
        mixed = list(parts)
        for c in range(chunks):
            if c & bit:
                continue
            a, b = parts[c], parts[c | bit]
            if 2 * bit == chunks:
                up = down = pltpu.roll(jnp.where(upper, a, b), LANES // 2, 1)
            else:
                up = pltpu.roll(b, bit * along, 1)
                down = pltpu.roll(a, LANES - bit * along, 1)
            mixed[c] = jnp.where(upper, up, a)
            mixed[c | bit] = jnp.where(upper, b, down)
        parts = mixed
        bit *= 2
    return parts


def swap_rows(parts, sub):
    bit = 1
    while bit < len(parts):
        upper = sub & bit != 0
        mixed = list(parts)
        for c in range(len(parts)):
            if c & bit:
                continue
            a, b = parts[c], parts[c | bit]
            both = jnp.where(upper, a, b)
            mixed[c] = jnp.where(upper, pltpu.roll(both, bit, 0), a)
            mixed[c | bit] = jnp.where(upper, b, pltpu.roll(both, 8 - bit, 0))
        parts = mixed
        bit *= 2
    return parts


def place_kernel(
    in_ref, out_hbm, stage, sem, *, width_x, width_y, rows, message, across, along, scale
):
    devices = width_x * width_y
    halves = across * along // LANES
    chunks = LANES // along
    groups = width_y // chunks
    sums = in_ref[pl.ds(halves * rows, devices, stride=message), :]
    inverse = 1.0 / (jnp.sum(sums) * scale + 1e-06)
    lane = lax.broadcasted_iota(jnp.int32, (1, LANES), 1)
    sub = lax.broadcasted_iota(jnp.int32, (8, 1), 0)
    outer, inner = stage.shape[1:3]
    tiles = width_x * groups
    for tile in range(tiles):
        heads = [(tile * chunks + c) * message for c in range(chunks)]
        for u in range(outer):
            if inner == RADIX:
                spans = [pl.ds(head + u, halves * inner, stride=outer) for head in heads]
                parts = [jnp.log(1.0 + in_ref[span, :] * inverse) for span in spans]
                parts = swap_rows(swap_chunks(parts, along, lane), sub)
                for q in range(inner):
                    stage[tile, u, q] = parts[q]
            else:
                for h in range(halves):
                    spans = [pl.ds(head + h * rows, inner) for head in heads]
                    parts = [jnp.log(1.0 + in_ref[span, :] * inverse) for span in spans]
                    parts = swap_chunks(parts, along, lane)
                    for a in range(chunks):
                        stage[tile, u, :, h * chunks + a, :] = parts[a]
        if tile % BATCH == BATCH - 1:
            for done in range(tile + 1 - BATCH, tile + 1):
                pltpu.make_async_copy(
                    stage.at[done],
                    out_hbm.at[:, :, done // groups, done % groups],
                    sem,
                ).start()
    pltpu.make_async_copy(stage, stage, sem).wait()


def local_call(spectra, resample_index, resample_weight, disp_phase, surface_block, devices):
    across, along, samples = spectra.shape
    count = across * along
    rows = KEEP * BLOCK // devices
    halves = count // LANES
    message = halves * rows + 1
    short = samples // RADIX
    terms = samples // 2 // RADIX
    pieces = samples // LANES
    hbm = pl.BlockSpec(memory_space=pltpu.HBM)
    vmem = pl.BlockSpec(memory_space=pltpu.VMEM)
    line = lambda dtype: jax.ShapeDtypeStruct((pieces, LANES), dtype)
    plan = pl.pallas_call(
        functools.partial(plan_kernel, samples=samples),
        out_shape=(
            jax.ShapeDtypeStruct((RADIX, terms, short), jnp.bfloat16),
            jax.ShapeDtypeStruct((pieces, WINDOW, 2 * LANES), jnp.bfloat16),
            line(jnp.int32),
            line(jnp.float32),
            line(jnp.float32),
            line(jnp.float32),
            line(jnp.int32),
            line(jnp.int32),
        ),
        in_specs=[hbm] * 3,
        out_specs=(vmem,) * 8,
        scratch_shapes=[
            pltpu.VMEM((pieces, LANES), jnp.int32),
            pltpu.VMEM((pieces, LANES), jnp.float32),
            pltpu.VMEM((pieces, LANES), jnp.float32),
            pltpu.SemaphoreType.DMA((3,)),
        ],
        cost_estimate=pl.CostEstimate(
            flops=COST, transcendentals=0, bytes_accessed=6 * RADIX * terms * short
        ),
        compiler_params=pltpu.CompilerParams(vmem_limit_bytes=8 << 20),
        name="plan",
    )(
        *(
            pltpu.with_memory_space_constraint(v.reshape(pieces, LANES), pltpu.HBM)
            for v in (resample_index, resample_weight, disp_phase)
        )
    )
    return pl.pallas_call(
        functools.partial(local_kernel, devices=devices, rows=rows, message=message),
        out_shape=jax.ShapeDtypeStruct((devices * message, LANES), jnp.float32),
        in_specs=[vmem] * 10,
        out_specs=vmem,
        scratch_shapes=[
            pltpu.VMEM((pieces, count, LANES), jnp.float32),
            pltpu.VMEM((pieces, count, LANES), jnp.float32),
            pltpu.VMEM((halves, RADIX, 2 * LANES, short), jnp.bfloat16),
            pltpu.VMEM((8, LANES), jnp.float32),
            pltpu.SMEM((2 * pieces,), jnp.int32),
        ],
        compiler_params=pltpu.CompilerParams(vmem_limit_bytes=LIMIT),
        name="local",
    )(plan[0], spectra.reshape(count, samples), *plan[1:], surface_block)


def place_call(moved, rows, width_x, width_y, across, along):
    devices = width_x * width_y
    count = across * along
    halves = count // LANES
    message = halves * rows + 1
    height, width = width_x * across, width_y * along
    groups = width // LANES
    vmem = pl.BlockSpec(memory_space=pltpu.VMEM)
    hbm = pl.BlockSpec(memory_space=pltpu.HBM)
    inner = rows if rows % RADIX else RADIX
    placed = pl.pallas_call(
        functools.partial(
            place_kernel,
            width_x=width_x,
            width_y=width_y,
            rows=rows,
            message=message,
            across=across,
            along=along,
            scale=1.0 / (count * KEEP * BLOCK * devices),
        ),
        out_shape=jax.ShapeDtypeStruct(
            (rows // inner, inner, height // 8, groups, 8, LANES), jnp.float32
        ),
        in_specs=[vmem],
        out_specs=hbm,
        scratch_shapes=[
            pltpu.VMEM(
                (width_x * groups, rows // inner, inner, 8, LANES), jnp.float32
            ),
            pltpu.SemaphoreType.DMA,
        ],
        compiler_params=pltpu.CompilerParams(vmem_limit_bytes=8 << 20),
        name="place",
    )(moved)
    placed = placed.reshape(rows, height // 8, groups, 8, LANES)
    return jnp.transpose(placed, (0, 1, 3, 2, 4)).reshape(rows, height, width)


def on_device(spectra, resample_index, resample_weight, disp_phase, surface_block):
    across, along, samples = spectra.shape
    width_x = lax.axis_size("gx")
    width_y = lax.axis_size("gy")
    devices = width_x * width_y
    rows = KEEP * BLOCK // devices
    sent = local_call(
        spectra, resample_index, resample_weight, disp_phase, surface_block, devices
    )
    moved = lax.all_to_all(
        sent.reshape(devices, -1, 1, LANES),
        ("gx", "gy"),
        split_axis=0,
        concat_axis=0,
        tiled=True,
    ).reshape(sent.shape)
    return place_call(moved, rows, width_x, width_y, across, along)


def solution(mesh):
    placed = (P("gx", "gy", None), P(), P(), P(), P("gx", "gy"))
    return jax.shard_map(
        on_device,
        mesh=mesh,
        in_specs=placed,
        out_specs=P(("gx", "gy"), None, None),
        check_vma=False,
    )
```

```python
import functools
import math

import jax
import jax.numpy as jnp
from jax import lax
from jax.experimental import pallas as pl
from jax.experimental.pallas import tpu as pltpu
from jax.sharding import PartitionSpec as P

BLOCK = 128
KEEP = 5
LANES = 128
RADIX = 4
WINDOW = 256
BATCH = 4
PAD = 8
LIMIT = 24 << 20
NT = (((1,), (1,)), ((), ()))


def circle(x):
    s = x * x
    cosine = jnp.full_like(x, 1.0 / math.factorial(18))
    sine = jnp.full_like(x, 1.0 / math.factorial(19))
    for k in range(8, -1, -1):
        cosine = 1.0 / math.factorial(2 * k) - s * cosine
        sine = 1.0 / math.factorial(2 * k + 1) - s * sine
    return cosine, sine * x


def unit_circle(turns, samples):
    x = (turns - samples // 2).astype(jnp.float32) * (2.0 * math.pi / samples)
    cosine, sine = circle(x)
    return -cosine, -sine


def place_in_message(r, rows):
    if rows % RADIX:
        return r
    return (r % RADIX) * (rows // RADIX) + r // RADIX


def local_kernel(
    spec_hbm, idx_hbm, w_hbm, phase_hbm, surf_hbm, out_ref,
    table, spec, picks, idx, weight, phase, surf, real, imag, fold, total, starts, sems,
    *, devices, rows, message,
):
    count, samples = spec_hbm.shape
    short = samples // RADIX
    depths = samples // 2
    terms = depths // RADIX
    per_block = BLOCK // RADIX
    blocks = depths // BLOCK
    pieces = samples // LANES
    quarter = pieces // RADIX
    halves = count // LANES

    small = [
        pltpu.make_async_copy(idx_hbm, idx, sems.at[0]),
        pltpu.make_async_copy(w_hbm, weight, sems.at[1]),
        pltpu.make_async_copy(phase_hbm, phase, sems.at[2]),
        pltpu.make_async_copy(surf_hbm, surf, sems.at[3]),
    ]
    large = pltpu.make_async_copy(spec_hbm, spec, sems.at[4])
    for copy in small:
        copy.start()
    large.start()

    sub = lax.broadcasted_iota(jnp.int32, (8, short // 2), 0)
    lane = 2 * lax.broadcasted_iota(jnp.int32, (8, short // 2), 1) + 1
    turn = 2 * samples
    bases = [
        unit_circle(((RADIX * sub + q) * lane) & (turn - 1), turn) for q in range(RADIX)
    ]
    for g8 in range(terms // 64):
        rot_c, rot_s = unit_circle((8 * RADIX * (8 * g8 + sub) * lane) & (turn - 1), turn)
        for k in range(0, 8, 2):
            for q in range(RADIX):
                bc, bs = bases[q]
                both = []
                for t in (k, k + 1):
                    rc, rs = rot_c[t : t + 1], rot_s[t : t + 1]
                    both.append((bc * rc - bs * rs, bs * rc + bc * rs))
                row = (8 * g8 + k) * 8
                table[q, row : row + 16, : short // 2] = jnp.concatenate(
                    [both[0][0], both[1][0]], axis=0
                ).astype(jnp.bfloat16)
                table[q, row : row + 16, short // 2 :] = jnp.concatenate(
                    [both[0][1], both[1][1]], axis=0
                ).astype(jnp.bfloat16)
    total[...] = jnp.zeros_like(total)

    for copy in small:
        copy.wait()
    piece = lax.broadcasted_iota(jnp.int32, idx.shape, 0)
    back = LANES - 1 - lax.broadcasted_iota(jnp.int32, idx.shape, 1)

    def mirrored(ref):
        v = ref[...]
        turned = jnp.take_along_axis(v, back, axis=1, mode="promise_in_bounds")
        return jnp.where(piece % quarter >= quarter // 2, turned, v)

    index = mirrored(idx)
    idx[...] = index
    low = jnp.min(index, axis=1, keepdims=True)
    first = jnp.minimum((low // LANES) * LANES, samples - WINDOW)
    high = jnp.max(index, axis=1, keepdims=True) + 2
    longest = jnp.max(high - first)
    steps = (high - first + (LANES - 1)) // LANES
    phases = mirrored(phase)
    phase[...] = phases
    cos_phase, sin_phase = circle(phases)
    ws = mirrored(weight)
    weight[...] = ws
    near_all = index - first

    source = lax.broadcasted_iota(jnp.int32, (WINDOW, LANES), 0).astype(jnp.bfloat16)

    def pick(near):
        hits = []
        for k in range(2):
            want = jnp.clip(near + k, -1, WINDOW).astype(jnp.bfloat16)
            hits.append(jnp.where(source == want, jnp.bfloat16(1), jnp.bfloat16(0)))
        return hits

    def finish(left, right, w, c, s):
        r = (1.0 - w) * left + w * right
        rounded = lambda v: v.astype(jnp.bfloat16).astype(jnp.float32)
        return rounded(r * c), rounded(r * s)

    for b in range(pieces):
        near = near_all[b : b + 1]
        picks[b, :, :LANES], picks[b, :, LANES:] = pick(near)
    large.wait()
    for b in range(pieces):
        row = slice(b, b + 1)
        lines = spec[:, pl.ds(pl.multiple_of(first[b, 0], LANES), WINDOW)]
        pair = jnp.dot(lines, picks[b], preferred_element_type=jnp.float32)
        real[b, :count], imag[b, :count] = finish(
            pair[:, :LANES], pair[:, LANES:], ws[row], cos_phase[row], sin_phase[row]
        )

    @pl.when(longest > WINDOW)
    def _():
        for b in range(pieces):
            starts[b] = first[b, 0]
            starts[pieces + b] = steps[b, 0]

        def redo(b, carry):
            @pl.when(starts[pieces + b] * LANES > WINDOW)
            def _():
                near = idx[pl.ds(b, 1), :]

                def step(i, pair):
                    k = pl.multiple_of(starts[b] + i * LANES, LANES)
                    hits = jnp.concatenate(pick(near - k), axis=1)[:LANES]
                    return pair + jnp.dot(
                        spec[:, pl.ds(k, LANES)],
                        hits,
                        preferred_element_type=jnp.float32,
                    )

                pair = lax.fori_loop(
                    0,
                    starts[pieces + b],
                    step,
                    jnp.zeros((count, 2 * LANES), jnp.float32),
                )
                c, s = circle(phase[pl.ds(b, 1), :])
                w = weight[pl.ds(b, 1), :]
                re, im = finish(pair[:, :LANES], pair[:, LANES:], w, c, s)
                real[b, pl.ds(0, count)] = re
                imag[b, pl.ds(0, count)] = im

            return carry

        lax.fori_loop(0, pieces, redo, 0)

    def fold_lines(h, r0):
        at = pl.ds(pl.multiple_of(h * LANES + r0, 16), 16)
        top = pl.ds(pl.multiple_of(r0, 16), 16)
        bottom = pl.ds(pl.multiple_of(LANES + r0, 16), 16)
        for t in range(quarter // 2):
            re, im, re_, im_ = [], [], [], []
            for p in range(RADIX):
                re.append(real[p * quarter + t, at])
                im.append(imag[p * quarter + t, at])
                u = (p + 1) * quarter - 1 - t
                re_.append(real[u, at])
                im_.append(imag[u, at])
            ar, ai = re[0] + re[2], im[0] + im[2]
            br, bi = re[0] - re[2], im[0] - im[2]
            cr, ci = re[1] + re[3], im[1] + im[3]
            dr, di = re[1] - re[3], im[1] - im[3]
            ar_, ai_ = re_[0] + re_[2], im_[0] + im_[2]
            br_, bi_ = re_[0] - re_[2], im_[0] - im_[2]
            cr_, ci_ = re_[1] + re_[3], im_[1] + im_[3]
            er_, di_ = re_[3] - re_[1], im_[1] - im_[3]
            yz = [
                (ar + cr, ai + ci, ar_ + cr_, ai_ + ci_, True),
                (br + di, bi - dr, bi_ + er_, br_ + di_, False),
                (ar - cr, ai - ci, cr_ - ar_, ci_ - ai_, True),
                (br - di, bi + dr, er_ - bi_, br_ - di_, True),
            ]
            left = slice(t * LANES, (t + 1) * LANES)
            right = slice(short // 2 + t * LANES, short // 2 + (t + 1) * LANES)
            for q, (yr, yi, zr, zi, plus) in enumerate(yz):
                even, odd = (yi + zi, yi - zi) if plus else (yi - zi, yi + zi)
                fold[h, q, top, left] = (yr + zr).astype(jnp.bfloat16)
                fold[h, q, top, right] = odd.astype(jnp.bfloat16)
                fold[h, q, bottom, left] = even.astype(jnp.bfloat16)
                fold[h, q, bottom, right] = (zr - yr).astype(jnp.bfloat16)

    per_half = LANES // surf.shape[1]

    def transform(h, q):
        lines_at = range(h * per_half, (h + 1) * per_half)
        surface = jnp.concatenate([surf[x : x + 1, :] for x in lines_at], axis=1)
        chosen = [surface == s for s in range(1, blocks - KEEP + 1)]
        depth = lax.dot_general(
            table[q], fold[h, q, : 2 * LANES], NT, preferred_element_type=jnp.float32
        )
        re, im = depth[:, :LANES], depth[:, LANES:]
        power = re * re + im * im
        for k in range(KEEP):
            kept = power[k * per_block : (k + 1) * per_block]
            for s, hit in enumerate(chosen, 1):
                there = power[(k + s) * per_block : (k + s + 1) * per_block]
                kept = jnp.where(hit, there, kept)
            total[...] += jnp.sum(kept.reshape(per_block // 8, 8, LANES), axis=0)
            places = []
            for m in range(per_block):
                r = (k * per_block + m) * RADIX + q
                inside = place_in_message(r % rows, rows)
                places.append((r // rows) * message + h * rows + inside)
            m = 0
            while m < per_block:
                stop = m + 1
                while stop % 8 and places[stop] == places[stop - 1] + 1:
                    stop += 1
                out_ref[places[m] : places[m] + stop - m, :] = kept[m:stop]
                m = stop

    for h in range(halves):
        for r0 in range(0, LANES, 16):
            fold_lines(h, r0)
        for q in range(RADIX):
            transform(h, q)

    partial = jnp.sum(total[...], axis=0, keepdims=True)
    for dest in range(devices):
        at = dest * message + halves * rows
        out_ref[at : at + 1, :] = partial


def swap_chunks(parts, along, lane):
    chunks = len(parts)
    bit = 1
    while bit < chunks:
        upper = (lane // along) & bit != 0
        mixed = list(parts)
        for c in range(chunks):
            if c & bit:
                continue
            a, b = parts[c], parts[c | bit]
            if 2 * bit == chunks:
                up = down = pltpu.roll(jnp.where(upper, a, b), LANES // 2, 1)
            else:
                up = pltpu.roll(b, bit * along, 1)
                down = pltpu.roll(a, LANES - bit * along, 1)
            mixed[c] = jnp.where(upper, up, a)
            mixed[c | bit] = jnp.where(upper, b, down)
        parts = mixed
        bit *= 2
    return parts


def swap_rows(parts, sub):
    bit = 1
    while bit < len(parts):
        upper = sub & bit != 0
        mixed = list(parts)
        for c in range(len(parts)):
            if c & bit:
                continue
            a, b = parts[c], parts[c | bit]
            both = jnp.where(upper, a, b)
            mixed[c] = jnp.where(upper, pltpu.roll(both, bit, 0), a)
            mixed[c | bit] = jnp.where(upper, b, pltpu.roll(both, 8 - bit, 0))
        parts = mixed
        bit *= 2
    return parts


def place_kernel(
    in_ref, out_hbm, stage, sem, *, width_x, width_y, rows, message, across, along, scale
):
    devices = width_x * width_y
    halves = across * along // LANES
    chunks = LANES // along
    groups = width_y // chunks
    sums = in_ref[pl.ds(halves * rows, devices, stride=message), :]
    inverse = 1.0 / (jnp.sum(sums) * scale + 1e-06)
    lane = lax.broadcasted_iota(jnp.int32, (1, LANES), 1)
    sub = lax.broadcasted_iota(jnp.int32, (8, 1), 0)
    outer, inner = stage.shape[1:3]
    tiles = width_x * groups
    for tile in range(tiles):
        heads = [(tile * chunks + c) * message for c in range(chunks)]
        for u in range(outer):
            if inner == RADIX:
                spans = [pl.ds(head + u, halves * inner, stride=outer) for head in heads]
                parts = [jnp.log(1.0 + in_ref[span, :] * inverse) for span in spans]
                parts = swap_rows(swap_chunks(parts, along, lane), sub)
                for q in range(inner):
                    stage[tile, u, q] = parts[q]
            else:
                for h in range(halves):
                    spans = [pl.ds(head + h * rows, inner) for head in heads]
                    parts = [jnp.log(1.0 + in_ref[span, :] * inverse) for span in spans]
                    parts = swap_chunks(parts, along, lane)
                    for a in range(chunks):
                        stage[tile, u, :, h * chunks + a, :] = parts[a]
        if tile % BATCH == BATCH - 1:
            for done in range(tile + 1 - BATCH, tile + 1):
                pltpu.make_async_copy(
                    stage.at[done],
                    out_hbm.at[:, :, done // groups, done % groups],
                    sem,
                ).start()
    pltpu.make_async_copy(stage, stage, sem).wait()


def local_call(spectra, resample_index, resample_weight, disp_phase, surface_block, devices):
    across, along, samples = spectra.shape
    count = across * along
    rows = KEEP * BLOCK // devices
    halves = count // LANES
    message = halves * rows + 1
    short = samples // RADIX
    terms = samples // 2 // RADIX
    pieces = samples // LANES
    vmem = pl.BlockSpec(memory_space=pltpu.VMEM)
    hbm = pl.BlockSpec(memory_space=pltpu.HBM)
    return pl.pallas_call(
        functools.partial(local_kernel, devices=devices, rows=rows, message=message),
        out_shape=jax.ShapeDtypeStruct((devices * message, LANES), jnp.float32),
        in_specs=[hbm] * 5,
        out_specs=vmem,
        scratch_shapes=[
            pltpu.VMEM((RADIX, terms, short), jnp.bfloat16),
            pltpu.VMEM((count, samples), jnp.bfloat16),
            pltpu.VMEM((pieces, WINDOW, 2 * LANES), jnp.bfloat16),
            pltpu.VMEM((pieces, LANES), jnp.int32),
            pltpu.VMEM((pieces, LANES), jnp.float32),
            pltpu.VMEM((pieces, LANES), jnp.float32),
            pltpu.VMEM((across, along), jnp.int32),
            pltpu.VMEM((pieces, count + PAD, LANES), jnp.float32),
            pltpu.VMEM((pieces, count + PAD, LANES), jnp.float32),
            pltpu.VMEM((halves, RADIX, 2 * LANES + 2 * PAD, short), jnp.bfloat16),
            pltpu.VMEM((8, LANES), jnp.float32),
            pltpu.SMEM((2 * pieces,), jnp.int32),
            pltpu.SemaphoreType.DMA((5,)),
        ],
        compiler_params=pltpu.CompilerParams(vmem_limit_bytes=LIMIT),
        name="local",
    )(
        *(
            pltpu.with_memory_space_constraint(v, pltpu.HBM)
            for v in (
                spectra.reshape(count, samples),
                resample_index.reshape(pieces, LANES),
                resample_weight.reshape(pieces, LANES),
                disp_phase.reshape(pieces, LANES),
                surface_block,
            )
        ),
    )


def place_call(moved, rows, width_x, width_y, across, along):
    devices = width_x * width_y
    count = across * along
    halves = count // LANES
    message = halves * rows + 1
    height, width = width_x * across, width_y * along
    groups = width // LANES
    vmem = pl.BlockSpec(memory_space=pltpu.VMEM)
    hbm = pl.BlockSpec(memory_space=pltpu.HBM)
    inner = rows if rows % RADIX else RADIX
    placed = pl.pallas_call(
        functools.partial(
            place_kernel,
            width_x=width_x,
            width_y=width_y,
            rows=rows,
            message=message,
            across=across,
            along=along,
            scale=1.0 / (count * KEEP * BLOCK * devices),
        ),
        out_shape=jax.ShapeDtypeStruct(
            (rows // inner, inner, height // 8, groups, 8, LANES), jnp.float32
        ),
        in_specs=[vmem],
        out_specs=hbm,
        scratch_shapes=[
            pltpu.VMEM(
                (width_x * groups, rows // inner, inner, 8, LANES), jnp.float32
            ),
            pltpu.SemaphoreType.DMA,
        ],
        compiler_params=pltpu.CompilerParams(vmem_limit_bytes=8 << 20),
        name="place",
    )(moved)
    placed = placed.reshape(rows, height // 8, groups, 8, LANES)
    return jnp.transpose(placed, (0, 1, 3, 2, 4)).reshape(rows, height, width)


def on_device(spectra, resample_index, resample_weight, disp_phase, surface_block):
    across, along, samples = spectra.shape
    width_x = lax.axis_size("gx")
    width_y = lax.axis_size("gy")
    devices = width_x * width_y
    rows = KEEP * BLOCK // devices
    sent = local_call(
        spectra, resample_index, resample_weight, disp_phase, surface_block, devices
    )
    moved = lax.all_to_all(
        sent.reshape(devices, -1, 1, LANES),
        ("gx", "gy"),
        split_axis=0,
        concat_axis=0,
        tiled=True,
    ).reshape(sent.shape)
    return place_call(moved, rows, width_x, width_y, across, along)


def solution(mesh):
    placed = (P("gx", "gy", None), P(), P(), P(), P("gx", "gy"))
    return jax.shard_map(
        on_device,
        mesh=mesh,
        in_specs=placed,
        out_specs=P(("gx", "gy"), None, None),
        check_vma=False,
    )
```

```python
import functools
import math

import jax
import jax.numpy as jnp
from jax import lax
from jax.experimental import pallas as pl
from jax.experimental.pallas import tpu as pltpu
from jax.sharding import PartitionSpec as P

BLOCK = 128
KEEP = 5
LANES = 128
RADIX = 4
WINDOW = 256
BATCH = 1
PAD = 8
LIMIT = 24 << 20
NT = (((1,), (1,)), ((), ()))


def circle(x):
    s = x * x
    cosine = jnp.full_like(x, 1.0 / math.factorial(18))
    sine = jnp.full_like(x, 1.0 / math.factorial(19))
    for k in range(8, -1, -1):
        cosine = 1.0 / math.factorial(2 * k) - s * cosine
        sine = 1.0 / math.factorial(2 * k + 1) - s * sine
    return cosine, sine * x


def unit_circle(turns, samples):
    x = (turns - samples // 2).astype(jnp.float32) * (2.0 * math.pi / samples)
    cosine, sine = circle(x)
    return -cosine, -sine


def place_in_message(r, rows):
    if rows % RADIX:
        return r
    return (r % RADIX) * (rows // RADIX) + r // RADIX


def local_kernel(
    spec_hbm, idx_hbm, w_hbm, phase_hbm, surf_hbm, out_ref,
    table, spec, picks, idx, weight, phase, surf, real, imag, fold, total, starts, sems,
    *, devices, rows, message,
):
    count, samples = spec_hbm.shape
    short = samples // RADIX
    depths = samples // 2
    terms = depths // RADIX
    per_block = BLOCK // RADIX
    blocks = depths // BLOCK
    pieces = samples // LANES
    quarter = pieces // RADIX
    halves = count // LANES

    small = [
        pltpu.make_async_copy(idx_hbm, idx, sems.at[0]),
        pltpu.make_async_copy(w_hbm, weight, sems.at[1]),
        pltpu.make_async_copy(phase_hbm, phase, sems.at[2]),
        pltpu.make_async_copy(surf_hbm, surf, sems.at[3]),
    ]
    large = pltpu.make_async_copy(spec_hbm, spec, sems.at[4])
    for copy in small:
        copy.start()
    large.start()

    sub = lax.broadcasted_iota(jnp.int32, (8, short // 2), 0)
    lane = 2 * lax.broadcasted_iota(jnp.int32, (8, short // 2), 1) + 1
    turn = 2 * samples
    bases = [
        unit_circle(((RADIX * sub + q) * lane) & (turn - 1), turn) for q in range(RADIX)
    ]
    for g8 in range(terms // 64):
        rot_c, rot_s = unit_circle((8 * RADIX * (8 * g8 + sub) * lane) & (turn - 1), turn)
        for k in range(0, 8, 2):
            for q in range(RADIX):
                bc, bs = bases[q]
                both = []
                for t in (k, k + 1):
                    rc, rs = rot_c[t : t + 1], rot_s[t : t + 1]
                    both.append((bc * rc - bs * rs, bs * rc + bc * rs))
                row = (8 * g8 + k) * 8
                table[q, row : row + 16, : short // 2] = jnp.concatenate(
                    [both[0][0], both[1][0]], axis=0
                ).astype(jnp.bfloat16)
                table[q, row : row + 16, short // 2 :] = jnp.concatenate(
                    [both[0][1], both[1][1]], axis=0
                ).astype(jnp.bfloat16)
    total[...] = jnp.zeros_like(total)

    for copy in small:
        copy.wait()
    piece = lax.broadcasted_iota(jnp.int32, idx.shape, 0)
    back = LANES - 1 - lax.broadcasted_iota(jnp.int32, idx.shape, 1)

    def mirrored(ref):
        v = ref[...]
        turned = jnp.take_along_axis(v, back, axis=1, mode="promise_in_bounds")
        return jnp.where(piece % quarter >= quarter // 2, turned, v)

    index = mirrored(idx)
    idx[...] = index
    low = jnp.min(index, axis=1, keepdims=True)
    first = jnp.minimum((low // LANES) * LANES, samples - WINDOW)
    high = jnp.max(index, axis=1, keepdims=True) + 2
    longest = jnp.max(high - first)
    steps = (high - first + (LANES - 1)) // LANES
    phases = mirrored(phase)
    phase[...] = phases
    cos_phase, sin_phase = circle(phases)
    ws = mirrored(weight)
    weight[...] = ws
    near_all = index - first

    source = lax.broadcasted_iota(jnp.int32, (WINDOW, LANES), 0).astype(jnp.bfloat16)

    def pick(near):
        hits = []
        for k in range(2):
            want = jnp.clip(near + k, -1, WINDOW).astype(jnp.bfloat16)
            hits.append(jnp.where(source == want, jnp.bfloat16(1), jnp.bfloat16(0)))
        return hits

    def finish(left, right, w, c, s):
        r = (1.0 - w) * left + w * right
        rounded = lambda v: v.astype(jnp.bfloat16).astype(jnp.float32)
        return rounded(r * c), rounded(r * s)

    for b in range(pieces):
        near = near_all[b : b + 1]
        picks[b, :, :LANES], picks[b, :, LANES:] = pick(near)
    large.wait()
    for b in range(pieces):
        row = slice(b, b + 1)
        lines = spec[:, pl.ds(pl.multiple_of(first[b, 0], LANES), WINDOW)]
        pair = jnp.dot(lines, picks[b], preferred_element_type=jnp.float32)
        real[b, :count], imag[b, :count] = finish(
            pair[:, :LANES], pair[:, LANES:], ws[row], cos_phase[row], sin_phase[row]
        )

    @pl.when(longest > WINDOW)
    def _():
        for b in range(pieces):
            starts[b] = first[b, 0]
            starts[pieces + b] = steps[b, 0]

        def redo(b, carry):
            @pl.when(starts[pieces + b] * LANES > WINDOW)
            def _():
                near = idx[pl.ds(b, 1), :]

                def step(i, pair):
                    k = pl.multiple_of(starts[b] + i * LANES, LANES)
                    hits = jnp.concatenate(pick(near - k), axis=1)[:LANES]
                    return pair + jnp.dot(
                        spec[:, pl.ds(k, LANES)],
                        hits,
                        preferred_element_type=jnp.float32,
                    )

                pair = lax.fori_loop(
                    0,
                    starts[pieces + b],
                    step,
                    jnp.zeros((count, 2 * LANES), jnp.float32),
                )
                c, s = circle(phase[pl.ds(b, 1), :])
                w = weight[pl.ds(b, 1), :]
                re, im = finish(pair[:, :LANES], pair[:, LANES:], w, c, s)
                real[b, pl.ds(0, count)] = re
                imag[b, pl.ds(0, count)] = im

            return carry

        lax.fori_loop(0, pieces, redo, 0)

    def fold_lines(h, r0):
        at = pl.ds(pl.multiple_of(h * LANES + r0, 16), 16)
        top = pl.ds(pl.multiple_of(r0, 16), 16)
        bottom = pl.ds(pl.multiple_of(LANES + r0, 16), 16)
        for t in range(quarter // 2):
            re, im, re_, im_ = [], [], [], []
            for p in range(RADIX):
                re.append(real[p * quarter + t, at])
                im.append(imag[p * quarter + t, at])
                u = (p + 1) * quarter - 1 - t
                re_.append(real[u, at])
                im_.append(imag[u, at])
            ar, ai = re[0] + re[2], im[0] + im[2]
            br, bi = re[0] - re[2], im[0] - im[2]
            cr, ci = re[1] + re[3], im[1] + im[3]
            dr, di = re[1] - re[3], im[1] - im[3]
            ar_, ai_ = re_[0] + re_[2], im_[0] + im_[2]
            br_, bi_ = re_[0] - re_[2], im_[0] - im_[2]
            cr_, ci_ = re_[1] + re_[3], im_[1] + im_[3]
            er_, di_ = re_[3] - re_[1], im_[1] - im_[3]
            yz = [
                (ar + cr, ai + ci, ar_ + cr_, ai_ + ci_, True),
                (br + di, bi - dr, bi_ + er_, br_ + di_, False),
                (ar - cr, ai - ci, cr_ - ar_, ci_ - ai_, True),
                (br - di, bi + dr, er_ - bi_, br_ - di_, True),
            ]
            left = slice(t * LANES, (t + 1) * LANES)
            right = slice(short // 2 + t * LANES, short // 2 + (t + 1) * LANES)
            for q, (yr, yi, zr, zi, plus) in enumerate(yz):
                even, odd = (yi + zi, yi - zi) if plus else (yi - zi, yi + zi)
                fold[h, q, top, left] = (yr + zr).astype(jnp.bfloat16)
                fold[h, q, top, right] = odd.astype(jnp.bfloat16)
                fold[h, q, bottom, left] = even.astype(jnp.bfloat16)
                fold[h, q, bottom, right] = (zr - yr).astype(jnp.bfloat16)

    per_half = LANES // surf.shape[1]

    def transform(h, q):
        lines_at = range(h * per_half, (h + 1) * per_half)
        surface = jnp.concatenate([surf[x : x + 1, :] for x in lines_at], axis=1)
        chosen = [surface == s for s in range(1, blocks - KEEP + 1)]
        depth = lax.dot_general(
            table[q], fold[h, q, : 2 * LANES], NT, preferred_element_type=jnp.float32
        )
        re, im = depth[:, :LANES], depth[:, LANES:]
        power = re * re + im * im
        for k in range(KEEP):
            kept = power[k * per_block : (k + 1) * per_block]
            for s, hit in enumerate(chosen, 1):
                there = power[(k + s) * per_block : (k + s + 1) * per_block]
                kept = jnp.where(hit, there, kept)
            total[...] += jnp.sum(kept.reshape(per_block // 8, 8, LANES), axis=0)
            places = []
            for m in range(per_block):
                r = (k * per_block + m) * RADIX + q
                inside = place_in_message(r % rows, rows)
                places.append((r // rows) * message + h * rows + inside)
            m = 0
            while m < per_block:
                stop = m + 1
                while stop % 8 and places[stop] == places[stop - 1] + 1:
                    stop += 1
                out_ref[places[m] : places[m] + stop - m, :] = kept[m:stop]
                m = stop

    for h in range(halves):
        for r0 in range(0, LANES, 16):
            fold_lines(h, r0)
        for q in range(RADIX):
            transform(h, q)

    partial = jnp.sum(total[...], axis=0, keepdims=True)
    for dest in range(devices):
        at = dest * message + halves * rows
        out_ref[at : at + 1, :] = partial


def swap_chunks(parts, along, lane):
    chunks = len(parts)
    bit = 1
    while bit < chunks:
        upper = (lane // along) & bit != 0
        mixed = list(parts)
        for c in range(chunks):
            if c & bit:
                continue
            a, b = parts[c], parts[c | bit]
            if 2 * bit == chunks:
                up = down = pltpu.roll(jnp.where(upper, a, b), LANES // 2, 1)
            else:
                up = pltpu.roll(b, bit * along, 1)
                down = pltpu.roll(a, LANES - bit * along, 1)
            mixed[c] = jnp.where(upper, up, a)
            mixed[c | bit] = jnp.where(upper, b, down)
        parts = mixed
        bit *= 2
    return parts


def swap_rows(parts, sub):
    bit = 1
    while bit < len(parts):
        upper = sub & bit != 0
        mixed = list(parts)
        for c in range(len(parts)):
            if c & bit:
                continue
            a, b = parts[c], parts[c | bit]
            both = jnp.where(upper, a, b)
            mixed[c] = jnp.where(upper, pltpu.roll(both, bit, 0), a)
            mixed[c | bit] = jnp.where(upper, b, pltpu.roll(both, 8 - bit, 0))
        parts = mixed
        bit *= 2
    return parts


def place_kernel(
    in_ref, out_hbm, stage, sem, *, width_x, width_y, rows, message, across, along, scale
):
    devices = width_x * width_y
    halves = across * along // LANES
    chunks = LANES // along
    groups = width_y // chunks
    sums = in_ref[pl.ds(halves * rows, devices, stride=message), :]
    inverse = 1.0 / (jnp.sum(sums) * scale + 1e-06)
    lane = lax.broadcasted_iota(jnp.int32, (1, LANES), 1)
    sub = lax.broadcasted_iota(jnp.int32, (8, 1), 0)
    outer, inner = stage.shape[1:3]
    tiles = width_x * groups
    for tile in range(tiles):
        heads = [(tile * chunks + c) * message for c in range(chunks)]
        for u in range(outer):
            if inner == RADIX:
                spans = [pl.ds(head + u, halves * inner, stride=outer) for head in heads]
                parts = [jnp.log(1.0 + in_ref[span, :] * inverse) for span in spans]
                parts = swap_rows(swap_chunks(parts, along, lane), sub)
                for q in range(inner):
                    stage[tile, u, q] = parts[q]
            else:
                for h in range(halves):
                    spans = [pl.ds(head + h * rows, inner) for head in heads]
                    parts = [jnp.log(1.0 + in_ref[span, :] * inverse) for span in spans]
                    parts = swap_chunks(parts, along, lane)
                    for a in range(chunks):
                        stage[tile, u, :, h * chunks + a, :] = parts[a]
        if tile % BATCH == BATCH - 1:
            for done in range(tile + 1 - BATCH, tile + 1):
                pltpu.make_async_copy(
                    stage.at[done],
                    out_hbm.at[:, :, done // groups, done % groups],
                    sem,
                ).start()
    pltpu.make_async_copy(stage, stage, sem).wait()


def local_call(spectra, resample_index, resample_weight, disp_phase, surface_block, devices):
    across, along, samples = spectra.shape
    count = across * along
    rows = KEEP * BLOCK // devices
    halves = count // LANES
    message = halves * rows + 1
    short = samples // RADIX
    terms = samples // 2 // RADIX
    pieces = samples // LANES
    vmem = pl.BlockSpec(memory_space=pltpu.VMEM)
    hbm = pl.BlockSpec(memory_space=pltpu.HBM)
    return pl.pallas_call(
        functools.partial(local_kernel, devices=devices, rows=rows, message=message),
        out_shape=jax.ShapeDtypeStruct((devices * message, LANES), jnp.float32),
        in_specs=[hbm] * 5,
        out_specs=vmem,
        scratch_shapes=[
            pltpu.VMEM((RADIX, terms, short), jnp.bfloat16),
            pltpu.VMEM((count, samples), jnp.bfloat16),
            pltpu.VMEM((pieces, WINDOW, 2 * LANES), jnp.bfloat16),
            pltpu.VMEM((pieces, LANES), jnp.int32),
            pltpu.VMEM((pieces, LANES), jnp.float32),
            pltpu.VMEM((pieces, LANES), jnp.float32),
            pltpu.VMEM((across, along), jnp.int32),
            pltpu.VMEM((pieces, count + PAD, LANES), jnp.float32),
            pltpu.VMEM((pieces, count + PAD, LANES), jnp.float32),
            pltpu.VMEM((halves, RADIX, 2 * LANES + 2 * PAD, short), jnp.bfloat16),
            pltpu.VMEM((8, LANES), jnp.float32),
            pltpu.SMEM((2 * pieces,), jnp.int32),
            pltpu.SemaphoreType.DMA((5,)),
        ],
        compiler_params=pltpu.CompilerParams(vmem_limit_bytes=LIMIT),
        name="local",
    )(
        *(
            pltpu.with_memory_space_constraint(v, pltpu.HBM)
            for v in (
                spectra.reshape(count, samples),
                resample_index.reshape(pieces, LANES),
                resample_weight.reshape(pieces, LANES),
                disp_phase.reshape(pieces, LANES),
                surface_block,
            )
        ),
    )


def place_call(moved, rows, width_x, width_y, across, along):
    devices = width_x * width_y
    count = across * along
    halves = count // LANES
    message = halves * rows + 1
    height, width = width_x * across, width_y * along
    groups = width // LANES
    vmem = pl.BlockSpec(memory_space=pltpu.VMEM)
    hbm = pl.BlockSpec(memory_space=pltpu.HBM)
    inner = rows if rows % RADIX else RADIX
    placed = pl.pallas_call(
        functools.partial(
            place_kernel,
            width_x=width_x,
            width_y=width_y,
            rows=rows,
            message=message,
            across=across,
            along=along,
            scale=1.0 / (count * KEEP * BLOCK * devices),
        ),
        out_shape=jax.ShapeDtypeStruct(
            (rows // inner, inner, height // 8, groups, 8, LANES), jnp.float32
        ),
        in_specs=[vmem],
        out_specs=hbm,
        scratch_shapes=[
            pltpu.VMEM(
                (width_x * groups, rows // inner, inner, 8, LANES), jnp.float32
            ),
            pltpu.SemaphoreType.DMA,
        ],
        compiler_params=pltpu.CompilerParams(vmem_limit_bytes=8 << 20),
        name="place",
    )(moved)
    placed = placed.reshape(rows, height // 8, groups, 8, LANES)
    return jnp.transpose(placed, (0, 1, 3, 2, 4)).reshape(rows, height, width)


def on_device(spectra, resample_index, resample_weight, disp_phase, surface_block):
    across, along, samples = spectra.shape
    width_x = lax.axis_size("gx")
    width_y = lax.axis_size("gy")
    devices = width_x * width_y
    rows = KEEP * BLOCK // devices
    sent = local_call(
        spectra, resample_index, resample_weight, disp_phase, surface_block, devices
    )
    moved = lax.all_to_all(
        sent.reshape(devices, -1, 1, LANES),
        ("gx", "gy"),
        split_axis=0,
        concat_axis=0,
        tiled=True,
    ).reshape(sent.shape)
    return place_call(moved, rows, width_x, width_y, across, along)


def solution(mesh):
    placed = (P("gx", "gy", None), P(), P(), P(), P("gx", "gy"))
    return jax.shard_map(
        on_device,
        mesh=mesh,
        in_specs=placed,
        out_specs=P(("gx", "gy"), None, None),
        check_vma=False,
    )
```

```python
import functools
import math

import jax
import jax.numpy as jnp
from jax import lax
from jax.experimental import pallas as pl
from jax.experimental.pallas import tpu as pltpu
from jax.sharding import PartitionSpec as P

BLOCK = 128
KEEP = 5
LANES = 128
RADIX = 4
WINDOW = 256
BATCH = 4
PAD = 8
LIMIT = 24 << 20
NT = (((1,), (1,)), ((), ()))


def circle(x):
    s = x * x
    cosine = jnp.full_like(x, 1.0 / math.factorial(18))
    sine = jnp.full_like(x, 1.0 / math.factorial(19))
    for k in range(8, -1, -1):
        cosine = 1.0 / math.factorial(2 * k) - s * cosine
        sine = 1.0 / math.factorial(2 * k + 1) - s * sine
    return cosine, sine * x


def unit_circle(turns, samples):
    x = (turns - samples // 2).astype(jnp.float32) * (2.0 * math.pi / samples)
    cosine, sine = circle(x)
    return -cosine, -sine


def place_in_message(r, rows):
    if rows % RADIX:
        return r
    return (r % RADIX) * (rows // RADIX) + r // RADIX


def local_kernel(
    spec_hbm, idx_hbm, w_hbm, phase_hbm, surf_hbm, out_ref,
    table, spec, picks, idx, weight, phase, surf, real, imag, fold, total, starts, sems,
    *, devices, rows, message,
):
    count, samples = spec_hbm.shape
    short = samples // RADIX
    depths = samples // 2
    terms = depths // RADIX
    per_block = BLOCK // RADIX
    blocks = depths // BLOCK
    pieces = samples // LANES
    quarter = pieces // RADIX
    halves = count // LANES

    small = [
        pltpu.make_async_copy(idx_hbm, idx, sems.at[0]),
        pltpu.make_async_copy(w_hbm, weight, sems.at[1]),
        pltpu.make_async_copy(phase_hbm, phase, sems.at[2]),
        pltpu.make_async_copy(surf_hbm, surf, sems.at[3]),
    ]
    large = pltpu.make_async_copy(spec_hbm, spec, sems.at[4])
    for copy in small:
        copy.start()
    large.start()

    sub = lax.broadcasted_iota(jnp.int32, (8, short // 2), 0)
    lane = 2 * lax.broadcasted_iota(jnp.int32, (8, short // 2), 1) + 1
    turn = 2 * samples
    bases = [
        unit_circle(((RADIX * sub + q) * lane) & (turn - 1), turn) for q in range(RADIX)
    ]
    for g8 in range(terms // 64):
        rot_c, rot_s = unit_circle((8 * RADIX * (8 * g8 + sub) * lane) & (turn - 1), turn)
        for k in range(0, 8, 2):
            for q in range(RADIX):
                bc, bs = bases[q]
                both = []
                for t in (k, k + 1):
                    rc, rs = rot_c[t : t + 1], rot_s[t : t + 1]
                    both.append((bc * rc - bs * rs, bs * rc + bc * rs))
                row = (8 * g8 + k) * 8
                table[q, row : row + 16, : short // 2] = jnp.concatenate(
                    [both[0][0], both[1][0]], axis=0
                ).astype(jnp.bfloat16)
                table[q, row : row + 16, short // 2 :] = jnp.concatenate(
                    [both[0][1], both[1][1]], axis=0
                ).astype(jnp.bfloat16)
    total[...] = jnp.zeros_like(total)

    for copy in small:
        copy.wait()
    piece = lax.broadcasted_iota(jnp.int32, idx.shape, 0)
    back = LANES - 1 - lax.broadcasted_iota(jnp.int32, idx.shape, 1)

    def mirrored(ref):
        v = ref[...]
        turned = jnp.take_along_axis(v, back, axis=1, mode="promise_in_bounds")
        return jnp.where(piece % quarter >= quarter // 2, turned, v)

    index = mirrored(idx)
    idx[...] = index
    low = jnp.min(index, axis=1, keepdims=True)
    first = jnp.minimum((low // LANES) * LANES, samples - WINDOW)
    high = jnp.max(index, axis=1, keepdims=True) + 2
    longest = jnp.max(high - first)
    steps = (high - first + (LANES - 1)) // LANES
    phases = mirrored(phase)
    phase[...] = phases
    cos_phase, sin_phase = circle(phases)
    ws = mirrored(weight)
    weight[...] = ws
    near_all = index - first

    source = lax.broadcasted_iota(jnp.int32, (WINDOW, LANES), 0).astype(jnp.bfloat16)

    def pick(near):
        hits = []
        for k in range(2):
            want = jnp.clip(near + k, -1, WINDOW).astype(jnp.bfloat16)
            hits.append(jnp.where(source == want, jnp.bfloat16(1), jnp.bfloat16(0)))
        return hits

    def finish(left, right, w, c, s):
        r = (1.0 - w) * left + w * right
        rounded = lambda v: v.astype(jnp.bfloat16).astype(jnp.float32)
        return rounded(r * c), rounded(r * s)

    for b in range(pieces):
        near = near_all[b : b + 1]
        picks[b, :WINDOW, :LANES], picks[b, :WINDOW, LANES:] = pick(near)
    large.wait()
    for b in range(pieces):
        row = slice(b, b + 1)
        lines = spec[:, pl.ds(pl.multiple_of(first[b, 0], LANES), WINDOW)]
        pair = jnp.dot(lines, picks[b, :WINDOW], preferred_element_type=jnp.float32)
        real[b, :count], imag[b, :count] = finish(
            pair[:, :LANES], pair[:, LANES:], ws[row], cos_phase[row], sin_phase[row]
        )

    @pl.when(longest > WINDOW)
    def _():
        for b in range(pieces):
            starts[b] = first[b, 0]
            starts[pieces + b] = steps[b, 0]

        def redo(b, carry):
            @pl.when(starts[pieces + b] * LANES > WINDOW)
            def _():
                near = idx[pl.ds(b, 1), :]

                def step(i, pair):
                    k = pl.multiple_of(starts[b] + i * LANES, LANES)
                    hits = jnp.concatenate(pick(near - k), axis=1)[:LANES]
                    return pair + jnp.dot(
                        spec[:, pl.ds(k, LANES)],
                        hits,
                        preferred_element_type=jnp.float32,
                    )

                pair = lax.fori_loop(
                    0,
                    starts[pieces + b],
                    step,
                    jnp.zeros((count, 2 * LANES), jnp.float32),
                )
                c, s = circle(phase[pl.ds(b, 1), :])
                w = weight[pl.ds(b, 1), :]
                re, im = finish(pair[:, :LANES], pair[:, LANES:], w, c, s)
                real[b, pl.ds(0, count)] = re
                imag[b, pl.ds(0, count)] = im

            return carry

        lax.fori_loop(0, pieces, redo, 0)

    def fold_lines(h, r0):
        at = pl.ds(pl.multiple_of(h * LANES + r0, 16), 16)
        top = pl.ds(pl.multiple_of(r0, 16), 16)
        bottom = pl.ds(pl.multiple_of(LANES + r0, 16), 16)
        for t in range(quarter // 2):
            re, im, re_, im_ = [], [], [], []
            for p in range(RADIX):
                re.append(real[p * quarter + t, at])
                im.append(imag[p * quarter + t, at])
                u = (p + 1) * quarter - 1 - t
                re_.append(real[u, at])
                im_.append(imag[u, at])
            ar, ai = re[0] + re[2], im[0] + im[2]
            br, bi = re[0] - re[2], im[0] - im[2]
            cr, ci = re[1] + re[3], im[1] + im[3]
            dr, di = re[1] - re[3], im[1] - im[3]
            ar_, ai_ = re_[0] + re_[2], im_[0] + im_[2]
            br_, bi_ = re_[0] - re_[2], im_[0] - im_[2]
            cr_, ci_ = re_[1] + re_[3], im_[1] + im_[3]
            er_, di_ = re_[3] - re_[1], im_[1] - im_[3]
            yz = [
                (ar + cr, ai + ci, ar_ + cr_, ai_ + ci_, True),
                (br + di, bi - dr, bi_ + er_, br_ + di_, False),
                (ar - cr, ai - ci, cr_ - ar_, ci_ - ai_, True),
                (br - di, bi + dr, er_ - bi_, br_ - di_, True),
            ]
            left = slice(t * LANES, (t + 1) * LANES)
            right = slice(short // 2 + t * LANES, short // 2 + (t + 1) * LANES)
            for q, (yr, yi, zr, zi, plus) in enumerate(yz):
                even, odd = (yi + zi, yi - zi) if plus else (yi - zi, yi + zi)
                fold[h, q, top, left] = (yr + zr).astype(jnp.bfloat16)
                fold[h, q, top, right] = odd.astype(jnp.bfloat16)
                fold[h, q, bottom, left] = even.astype(jnp.bfloat16)
                fold[h, q, bottom, right] = (zr - yr).astype(jnp.bfloat16)

    per_half = LANES // surf.shape[1]

    def transform(h, q):
        lines_at = range(h * per_half, (h + 1) * per_half)
        surface = jnp.concatenate([surf[x : x + 1, :] for x in lines_at], axis=1)
        chosen = [surface == s for s in range(1, blocks - KEEP + 1)]
        depth = lax.dot_general(
            table[q, :terms], fold[h, q, : 2 * LANES], NT, preferred_element_type=jnp.float32
        )
        re, im = depth[:, :LANES], depth[:, LANES:]
        power = re * re + im * im
        for k in range(KEEP):
            kept = power[k * per_block : (k + 1) * per_block]
            for s, hit in enumerate(chosen, 1):
                there = power[(k + s) * per_block : (k + s + 1) * per_block]
                kept = jnp.where(hit, there, kept)
            total[...] += jnp.sum(kept.reshape(per_block // 8, 8, LANES), axis=0)
            places = []
            for m in range(per_block):
                r = (k * per_block + m) * RADIX + q
                inside = place_in_message(r % rows, rows)
                places.append((r // rows) * message + h * rows + inside)
            m = 0
            while m < per_block:
                stop = m + 1
                while stop % 8 and places[stop] == places[stop - 1] + 1:
                    stop += 1
                out_ref[places[m] : places[m] + stop - m, :] = kept[m:stop]
                m = stop

    for h in range(halves):
        for r0 in range(0, LANES, 16):
            fold_lines(h, r0)
        for q in range(RADIX):
            transform(h, q)

    partial = jnp.sum(total[...], axis=0, keepdims=True)
    for dest in range(devices):
        at = dest * message + halves * rows
        out_ref[at : at + 1, :] = partial


def swap_chunks(parts, along, lane):
    chunks = len(parts)
    bit = 1
    while bit < chunks:
        upper = (lane // along) & bit != 0
        mixed = list(parts)
        for c in range(chunks):
            if c & bit:
                continue
            a, b = parts[c], parts[c | bit]
            if 2 * bit == chunks:
                up = down = pltpu.roll(jnp.where(upper, a, b), LANES // 2, 1)
            else:
                up = pltpu.roll(b, bit * along, 1)
                down = pltpu.roll(a, LANES - bit * along, 1)
            mixed[c] = jnp.where(upper, up, a)
            mixed[c | bit] = jnp.where(upper, b, down)
        parts = mixed
        bit *= 2
    return parts


def swap_rows(parts, sub):
    bit = 1
    while bit < len(parts):
        upper = sub & bit != 0
        mixed = list(parts)
        for c in range(len(parts)):
            if c & bit:
                continue
            a, b = parts[c], parts[c | bit]
            both = jnp.where(upper, a, b)
            mixed[c] = jnp.where(upper, pltpu.roll(both, bit, 0), a)
            mixed[c | bit] = jnp.where(upper, b, pltpu.roll(both, 8 - bit, 0))
        parts = mixed
        bit *= 2
    return parts


def place_kernel(
    in_ref, out_hbm, stage, sem, *, width_x, width_y, rows, message, across, along, scale
):
    devices = width_x * width_y
    halves = across * along // LANES
    chunks = LANES // along
    groups = width_y // chunks
    sums = in_ref[pl.ds(halves * rows, devices, stride=message), :]
    inverse = 1.0 / (jnp.sum(sums) * scale + 1e-06)
    lane = lax.broadcasted_iota(jnp.int32, (1, LANES), 1)
    sub = lax.broadcasted_iota(jnp.int32, (8, 1), 0)
    outer, inner = stage.shape[1:3]
    tiles = width_x * groups
    for tile in range(tiles):
        heads = [(tile * chunks + c) * message for c in range(chunks)]
        for u in range(outer):
            if inner == RADIX:
                spans = [pl.ds(head + u, halves * inner, stride=outer) for head in heads]
                parts = [jnp.log(1.0 + in_ref[span, :] * inverse) for span in spans]
                parts = swap_rows(swap_chunks(parts, along, lane), sub)
                for q in range(inner):
                    stage[tile, u, q] = parts[q]
            else:
                for h in range(halves):
                    spans = [pl.ds(head + h * rows, inner) for head in heads]
                    parts = [jnp.log(1.0 + in_ref[span, :] * inverse) for span in spans]
                    parts = swap_chunks(parts, along, lane)
                    for a in range(chunks):
                        stage[tile, u, :, h * chunks + a, :] = parts[a]
        if tile % BATCH == BATCH - 1:
            for done in range(tile + 1 - BATCH, tile + 1):
                pltpu.make_async_copy(
                    stage.at[done],
                    out_hbm.at[:, :, done // groups, done % groups],
                    sem,
                ).start()
    pltpu.make_async_copy(stage, stage, sem).wait()


def local_call(spectra, resample_index, resample_weight, disp_phase, surface_block, devices):
    across, along, samples = spectra.shape
    count = across * along
    rows = KEEP * BLOCK // devices
    halves = count // LANES
    message = halves * rows + 1
    short = samples // RADIX
    terms = samples // 2 // RADIX
    pieces = samples // LANES
    vmem = pl.BlockSpec(memory_space=pltpu.VMEM)
    hbm = pl.BlockSpec(memory_space=pltpu.HBM)
    return pl.pallas_call(
        functools.partial(local_kernel, devices=devices, rows=rows, message=message),
        out_shape=jax.ShapeDtypeStruct((devices * message, LANES), jnp.float32),
        in_specs=[hbm] * 5,
        out_specs=vmem,
        scratch_shapes=[
            pltpu.VMEM((RADIX, terms + 2 * PAD, short), jnp.bfloat16),
            pltpu.VMEM((count, samples), jnp.bfloat16),
            pltpu.VMEM((pieces, WINDOW + 2 * PAD, 2 * LANES), jnp.bfloat16),
            pltpu.VMEM((pieces, LANES), jnp.int32),
            pltpu.VMEM((pieces, LANES), jnp.float32),
            pltpu.VMEM((pieces, LANES), jnp.float32),
            pltpu.VMEM((across, along), jnp.int32),
            pltpu.VMEM((pieces, count + PAD, LANES), jnp.float32),
            pltpu.VMEM((pieces, count + PAD, LANES), jnp.float32),
            pltpu.VMEM((halves, RADIX, 2 * LANES + 2 * PAD, short), jnp.bfloat16),
            pltpu.VMEM((8, LANES), jnp.float32),
            pltpu.SMEM((2 * pieces,), jnp.int32),
            pltpu.SemaphoreType.DMA((5,)),
        ],
        compiler_params=pltpu.CompilerParams(vmem_limit_bytes=LIMIT),
        name="local",
    )(
        *(
            pltpu.with_memory_space_constraint(v, pltpu.HBM)
            for v in (
                spectra.reshape(count, samples),
                resample_index.reshape(pieces, LANES),
                resample_weight.reshape(pieces, LANES),
                disp_phase.reshape(pieces, LANES),
                surface_block,
            )
        ),
    )


def place_call(moved, rows, width_x, width_y, across, along):
    devices = width_x * width_y
    count = across * along
    halves = count // LANES
    message = halves * rows + 1
    height, width = width_x * across, width_y * along
    groups = width // LANES
    vmem = pl.BlockSpec(memory_space=pltpu.VMEM)
    hbm = pl.BlockSpec(memory_space=pltpu.HBM)
    inner = rows if rows % RADIX else RADIX
    placed = pl.pallas_call(
        functools.partial(
            place_kernel,
            width_x=width_x,
            width_y=width_y,
            rows=rows,
            message=message,
            across=across,
            along=along,
            scale=1.0 / (count * KEEP * BLOCK * devices),
        ),
        out_shape=jax.ShapeDtypeStruct(
            (rows // inner, inner, height // 8, groups, 8, LANES), jnp.float32
        ),
        in_specs=[vmem],
        out_specs=hbm,
        scratch_shapes=[
            pltpu.VMEM(
                (width_x * groups, rows // inner, inner, 8, LANES), jnp.float32
            ),
            pltpu.SemaphoreType.DMA,
        ],
        compiler_params=pltpu.CompilerParams(vmem_limit_bytes=8 << 20),
        name="place",
    )(moved)
    placed = placed.reshape(rows, height // 8, groups, 8, LANES)
    return jnp.transpose(placed, (0, 1, 3, 2, 4)).reshape(rows, height, width)


def on_device(spectra, resample_index, resample_weight, disp_phase, surface_block):
    across, along, samples = spectra.shape
    width_x = lax.axis_size("gx")
    width_y = lax.axis_size("gy")
    devices = width_x * width_y
    rows = KEEP * BLOCK // devices
    sent = local_call(
        spectra, resample_index, resample_weight, disp_phase, surface_block, devices
    )
    moved = lax.all_to_all(
        sent.reshape(devices, -1, 1, LANES),
        ("gx", "gy"),
        split_axis=0,
        concat_axis=0,
        tiled=True,
    ).reshape(sent.shape)
    return place_call(moved, rows, width_x, width_y, across, along)


def solution(mesh):
    placed = (P("gx", "gy", None), P(), P(), P(), P("gx", "gy"))
    return jax.shard_map(
        on_device,
        mesh=mesh,
        in_specs=placed,
        out_specs=P(("gx", "gy"), None, None),
        check_vma=False,
    )
```

```python
import functools
import math

import jax
import jax.numpy as jnp
from jax import lax
from jax.experimental import pallas as pl
from jax.experimental.pallas import tpu as pltpu
from jax.sharding import PartitionSpec as P

BLOCK = 128
KEEP = 5
LANES = 128
RADIX = 4
WINDOW = 256
BATCH = 2
PAD = 24
LIMIT = 24 << 20
NT = (((1,), (1,)), ((), ()))


def circle(x):
    s = x * x
    cosine = jnp.full_like(x, 1.0 / math.factorial(18))
    sine = jnp.full_like(x, 1.0 / math.factorial(19))
    for k in range(8, -1, -1):
        cosine = 1.0 / math.factorial(2 * k) - s * cosine
        sine = 1.0 / math.factorial(2 * k + 1) - s * sine
    return cosine, sine * x


def unit_circle(turns, samples):
    x = (turns - samples // 2).astype(jnp.float32) * (2.0 * math.pi / samples)
    cosine, sine = circle(x)
    return -cosine, -sine


def place_in_message(r, rows):
    if rows % RADIX:
        return r
    return (r % RADIX) * (rows // RADIX) + r // RADIX


def local_kernel(
    spec_hbm, idx_hbm, w_hbm, phase_hbm, surf_hbm, out_ref,
    table, spec, picks, idx, weight, phase, surf, real, imag, fold, total, starts, sems,
    *, devices, rows, message,
):
    count, samples = spec_hbm.shape
    short = samples // RADIX
    depths = samples // 2
    terms = depths // RADIX
    per_block = BLOCK // RADIX
    blocks = depths // BLOCK
    pieces = samples // LANES
    quarter = pieces // RADIX
    halves = count // LANES

    small = [
        pltpu.make_async_copy(idx_hbm, idx, sems.at[0]),
        pltpu.make_async_copy(w_hbm, weight, sems.at[1]),
        pltpu.make_async_copy(phase_hbm, phase, sems.at[2]),
        pltpu.make_async_copy(surf_hbm, surf, sems.at[3]),
    ]
    large = pltpu.make_async_copy(spec_hbm, spec, sems.at[4])
    for copy in small:
        copy.start()
    large.start()

    sub = lax.broadcasted_iota(jnp.int32, (8, short // 2), 0)
    lane = 2 * lax.broadcasted_iota(jnp.int32, (8, short // 2), 1) + 1
    turn = 2 * samples
    bases = [
        unit_circle(((RADIX * sub + q) * lane) & (turn - 1), turn) for q in range(RADIX)
    ]
    for g8 in range(terms // 64):
        rot_c, rot_s = unit_circle((8 * RADIX * (8 * g8 + sub) * lane) & (turn - 1), turn)
        for k in range(0, 8, 2):
            for q in range(RADIX):
                bc, bs = bases[q]
                both = []
                for t in (k, k + 1):
                    rc, rs = rot_c[t : t + 1], rot_s[t : t + 1]
                    both.append((bc * rc - bs * rs, bs * rc + bc * rs))
                row = (8 * g8 + k) * 8
                table[q, row : row + 16, : short // 2] = jnp.concatenate(
                    [both[0][0], both[1][0]], axis=0
                ).astype(jnp.bfloat16)
                table[q, row : row + 16, short // 2 :] = jnp.concatenate(
                    [both[0][1], both[1][1]], axis=0
                ).astype(jnp.bfloat16)
    total[...] = jnp.zeros_like(total)

    for copy in small:
        copy.wait()
    piece = lax.broadcasted_iota(jnp.int32, idx.shape, 0)
    back = LANES - 1 - lax.broadcasted_iota(jnp.int32, idx.shape, 1)

    def mirrored(ref):
        v = ref[...]
        turned = jnp.take_along_axis(v, back, axis=1, mode="promise_in_bounds")
        return jnp.where(piece % quarter >= quarter // 2, turned, v)

    index = mirrored(idx)
    idx[...] = index
    low = jnp.min(index, axis=1, keepdims=True)
    first = jnp.minimum((low // LANES) * LANES, samples - WINDOW)
    high = jnp.max(index, axis=1, keepdims=True) + 2
    longest = jnp.max(high - first)
    steps = (high - first + (LANES - 1)) // LANES
    phases = mirrored(phase)
    phase[...] = phases
    cos_phase, sin_phase = circle(phases)
    ws = mirrored(weight)
    weight[...] = ws
    near_all = index - first

    source = lax.broadcasted_iota(jnp.int32, (WINDOW, LANES), 0).astype(jnp.bfloat16)

    def pick(near):
        hits = []
        for k in range(2):
            want = jnp.clip(near + k, -1, WINDOW).astype(jnp.bfloat16)
            hits.append(jnp.where(source == want, jnp.bfloat16(1), jnp.bfloat16(0)))
        return hits

    def finish(left, right, w, c, s):
        r = (1.0 - w) * left + w * right
        rounded = lambda v: v.astype(jnp.bfloat16).astype(jnp.float32)
        return rounded(r * c), rounded(r * s)

    for b in range(pieces):
        near = near_all[b : b + 1]
        picks[b, :WINDOW, :LANES], picks[b, :WINDOW, LANES:] = pick(near)
    large.wait()
    for b in range(pieces):
        row = slice(b, b + 1)
        lines = spec[:, pl.ds(pl.multiple_of(first[b, 0], LANES), WINDOW)]
        pair = jnp.dot(lines, picks[b, :WINDOW], preferred_element_type=jnp.float32)
        real[b, :count], imag[b, :count] = finish(
            pair[:, :LANES], pair[:, LANES:], ws[row], cos_phase[row], sin_phase[row]
        )

    @pl.when(longest > WINDOW)
    def _():
        for b in range(pieces):
            starts[b] = first[b, 0]
            starts[pieces + b] = steps[b, 0]

        def redo(b, carry):
            @pl.when(starts[pieces + b] * LANES > WINDOW)
            def _():
                near = idx[pl.ds(b, 1), :]

                def step(i, pair):
                    k = pl.multiple_of(starts[b] + i * LANES, LANES)
                    hits = jnp.concatenate(pick(near - k), axis=1)[:LANES]
                    return pair + jnp.dot(
                        spec[:, pl.ds(k, LANES)],
                        hits,
                        preferred_element_type=jnp.float32,
                    )

                pair = lax.fori_loop(
                    0,
                    starts[pieces + b],
                    step,
                    jnp.zeros((count, 2 * LANES), jnp.float32),
                )
                c, s = circle(phase[pl.ds(b, 1), :])
                w = weight[pl.ds(b, 1), :]
                re, im = finish(pair[:, :LANES], pair[:, LANES:], w, c, s)
                real[b, pl.ds(0, count)] = re
                imag[b, pl.ds(0, count)] = im

            return carry

        lax.fori_loop(0, pieces, redo, 0)

    def fold_lines(h, r0):
        at = pl.ds(pl.multiple_of(h * LANES + r0, 16), 16)
        top = pl.ds(pl.multiple_of(r0, 16), 16)
        bottom = pl.ds(pl.multiple_of(LANES + r0, 16), 16)
        for t in range(quarter // 2):
            re, im, re_, im_ = [], [], [], []
            for p in range(RADIX):
                re.append(real[p * quarter + t, at])
                im.append(imag[p * quarter + t, at])
                u = (p + 1) * quarter - 1 - t
                re_.append(real[u, at])
                im_.append(imag[u, at])
            ar, ai = re[0] + re[2], im[0] + im[2]
            br, bi = re[0] - re[2], im[0] - im[2]
            cr, ci = re[1] + re[3], im[1] + im[3]
            dr, di = re[1] - re[3], im[1] - im[3]
            ar_, ai_ = re_[0] + re_[2], im_[0] + im_[2]
            br_, bi_ = re_[0] - re_[2], im_[0] - im_[2]
            cr_, ci_ = re_[1] + re_[3], im_[1] + im_[3]
            er_, di_ = re_[3] - re_[1], im_[1] - im_[3]
            yz = [
                (ar + cr, ai + ci, ar_ + cr_, ai_ + ci_, True),
                (br + di, bi - dr, bi_ + er_, br_ + di_, False),
                (ar - cr, ai - ci, cr_ - ar_, ci_ - ai_, True),
                (br - di, bi + dr, er_ - bi_, br_ - di_, True),
            ]
            left = slice(t * LANES, (t + 1) * LANES)
            right = slice(short // 2 + t * LANES, short // 2 + (t + 1) * LANES)
            for q, (yr, yi, zr, zi, plus) in enumerate(yz):
                even, odd = (yi + zi, yi - zi) if plus else (yi - zi, yi + zi)
                fold[h, q, top, left] = (yr + zr).astype(jnp.bfloat16)
                fold[h, q, top, right] = odd.astype(jnp.bfloat16)
                fold[h, q, bottom, left] = even.astype(jnp.bfloat16)
                fold[h, q, bottom, right] = (zr - yr).astype(jnp.bfloat16)

    per_half = LANES // surf.shape[1]

    def transform(h, q):
        lines_at = range(h * per_half, (h + 1) * per_half)
        surface = jnp.concatenate([surf[x : x + 1, :] for x in lines_at], axis=1)
        chosen = [surface == s for s in range(1, blocks - KEEP + 1)]
        depth = lax.dot_general(
            table[q, :terms], fold[h, q, : 2 * LANES], NT, preferred_element_type=jnp.float32
        )
        re, im = depth[:, :LANES], depth[:, LANES:]
        power = re * re + im * im
        for k in range(KEEP):
            kept = power[k * per_block : (k + 1) * per_block]
            for s, hit in enumerate(chosen, 1):
                there = power[(k + s) * per_block : (k + s + 1) * per_block]
                kept = jnp.where(hit, there, kept)
            total[...] += jnp.sum(kept.reshape(per_block // 8, 8, LANES), axis=0)
            places = []
            for m in range(per_block):
                r = (k * per_block + m) * RADIX + q
                inside = place_in_message(r % rows, rows)
                places.append((r // rows) * message + h * rows + inside)
            m = 0
            while m < per_block:
                stop = m + 1
                while stop % 8 and places[stop] == places[stop - 1] + 1:
                    stop += 1
                out_ref[places[m] : places[m] + stop - m, :] = kept[m:stop]
                m = stop

    for h in range(halves):
        for r0 in range(0, LANES, 16):
            fold_lines(h, r0)
        for q in range(RADIX):
            transform(h, q)

    partial = jnp.sum(total[...], axis=0, keepdims=True)
    for dest in range(devices):
        at = dest * message + halves * rows
        out_ref[at : at + 1, :] = partial


def swap_chunks(parts, along, lane):
    chunks = len(parts)
    bit = 1
    while bit < chunks:
        upper = (lane // along) & bit != 0
        mixed = list(parts)
        for c in range(chunks):
            if c & bit:
                continue
            a, b = parts[c], parts[c | bit]
            if 2 * bit == chunks:
                up = down = pltpu.roll(jnp.where(upper, a, b), LANES // 2, 1)
            else:
                up = pltpu.roll(b, bit * along, 1)
                down = pltpu.roll(a, LANES - bit * along, 1)
            mixed[c] = jnp.where(upper, up, a)
            mixed[c | bit] = jnp.where(upper, b, down)
        parts = mixed
        bit *= 2
    return parts


def swap_rows(parts, sub):
    bit = 1
    while bit < len(parts):
        upper = sub & bit != 0
        mixed = list(parts)
        for c in range(len(parts)):
            if c & bit:
                continue
            a, b = parts[c], parts[c | bit]
            both = jnp.where(upper, a, b)
            mixed[c] = jnp.where(upper, pltpu.roll(both, bit, 0), a)
            mixed[c | bit] = jnp.where(upper, b, pltpu.roll(both, 8 - bit, 0))
        parts = mixed
        bit *= 2
    return parts


def place_kernel(
    in_ref, out_hbm, stage, sem, *, width_x, width_y, rows, message, across, along, scale
):
    devices = width_x * width_y
    halves = across * along // LANES
    chunks = LANES // along
    groups = width_y // chunks
    sums = in_ref[pl.ds(halves * rows, devices, stride=message), :]
    inverse = 1.0 / (jnp.sum(sums) * scale + 1e-06)
    lane = lax.broadcasted_iota(jnp.int32, (1, LANES), 1)
    sub = lax.broadcasted_iota(jnp.int32, (8, 1), 0)
    outer, inner = stage.shape[1:3]
    tiles = width_x * groups
    for tile in range(tiles):
        heads = [(tile * chunks + c) * message for c in range(chunks)]
        for u in range(outer):
            if inner == RADIX:
                spans = [pl.ds(head + u, halves * inner, stride=outer) for head in heads]
                parts = [jnp.log(1.0 + in_ref[span, :] * inverse) for span in spans]
                parts = swap_rows(swap_chunks(parts, along, lane), sub)
                for q in range(inner):
                    stage[tile, u, q] = parts[q]
            else:
                for h in range(halves):
                    spans = [pl.ds(head + h * rows, inner) for head in heads]
                    parts = [jnp.log(1.0 + in_ref[span, :] * inverse) for span in spans]
                    parts = swap_chunks(parts, along, lane)
                    for a in range(chunks):
                        stage[tile, u, :, h * chunks + a, :] = parts[a]
        if tile % BATCH == BATCH - 1:
            for done in range(tile + 1 - BATCH, tile + 1):
                pltpu.make_async_copy(
                    stage.at[done],
                    out_hbm.at[:, :, done // groups, done % groups],
                    sem,
                ).start()
    pltpu.make_async_copy(stage, stage, sem).wait()


def local_call(spectra, resample_index, resample_weight, disp_phase, surface_block, devices):
    across, along, samples = spectra.shape
    count = across * along
    rows = KEEP * BLOCK // devices
    halves = count // LANES
    message = halves * rows + 1
    short = samples // RADIX
    terms = samples // 2 // RADIX
    pieces = samples // LANES
    vmem = pl.BlockSpec(memory_space=pltpu.VMEM)
    hbm = pl.BlockSpec(memory_space=pltpu.HBM)
    return pl.pallas_call(
        functools.partial(local_kernel, devices=devices, rows=rows, message=message),
        out_shape=jax.ShapeDtypeStruct((devices * message, LANES), jnp.float32),
        in_specs=[hbm] * 5,
        out_specs=vmem,
        scratch_shapes=[
            pltpu.VMEM((RADIX, terms + 2 * PAD, short), jnp.bfloat16),
            pltpu.VMEM((count, samples), jnp.bfloat16),
            pltpu.VMEM((pieces, WINDOW + 2 * PAD, 2 * LANES), jnp.bfloat16),
            pltpu.VMEM((pieces, LANES), jnp.int32),
            pltpu.VMEM((pieces, LANES), jnp.float32),
            pltpu.VMEM((pieces, LANES), jnp.float32),
            pltpu.VMEM((across, along), jnp.int32),
            pltpu.VMEM((pieces, count + PAD, LANES), jnp.float32),
            pltpu.VMEM((pieces, count + PAD, LANES), jnp.float32),
            pltpu.VMEM((halves, RADIX, 2 * LANES + 2 * PAD, short), jnp.bfloat16),
            pltpu.VMEM((8, LANES), jnp.float32),
            pltpu.SMEM((2 * pieces,), jnp.int32),
            pltpu.SemaphoreType.DMA((5,)),
        ],
        compiler_params=pltpu.CompilerParams(vmem_limit_bytes=LIMIT),
        name="local",
    )(
        *(
            pltpu.with_memory_space_constraint(v, pltpu.HBM)
            for v in (
                spectra.reshape(count, samples),
                resample_index.reshape(pieces, LANES),
                resample_weight.reshape(pieces, LANES),
                disp_phase.reshape(pieces, LANES),
                surface_block,
            )
        ),
    )


def place_call(moved, rows, width_x, width_y, across, along):
    devices = width_x * width_y
    count = across * along
    halves = count // LANES
    message = halves * rows + 1
    height, width = width_x * across, width_y * along
    groups = width // LANES
    vmem = pl.BlockSpec(memory_space=pltpu.VMEM)
    hbm = pl.BlockSpec(memory_space=pltpu.HBM)
    inner = rows if rows % RADIX else RADIX
    placed = pl.pallas_call(
        functools.partial(
            place_kernel,
            width_x=width_x,
            width_y=width_y,
            rows=rows,
            message=message,
            across=across,
            along=along,
            scale=1.0 / (count * KEEP * BLOCK * devices),
        ),
        out_shape=jax.ShapeDtypeStruct(
            (rows // inner, inner, height // 8, groups, 8, LANES), jnp.float32
        ),
        in_specs=[vmem],
        out_specs=hbm,
        scratch_shapes=[
            pltpu.VMEM(
                (width_x * groups, rows // inner, inner, 8, LANES), jnp.float32
            ),
            pltpu.SemaphoreType.DMA,
        ],
        compiler_params=pltpu.CompilerParams(vmem_limit_bytes=8 << 20),
        name="place",
    )(moved)
    placed = placed.reshape(rows, height // 8, groups, 8, LANES)
    return jnp.transpose(placed, (0, 1, 3, 2, 4)).reshape(rows, height, width)


def on_device(spectra, resample_index, resample_weight, disp_phase, surface_block):
    across, along, samples = spectra.shape
    width_x = lax.axis_size("gx")
    width_y = lax.axis_size("gy")
    devices = width_x * width_y
    rows = KEEP * BLOCK // devices
    sent = local_call(
        spectra, resample_index, resample_weight, disp_phase, surface_block, devices
    )
    moved = lax.all_to_all(
        sent.reshape(devices, -1, 1, LANES),
        ("gx", "gy"),
        split_axis=0,
        concat_axis=0,
        tiled=True,
    ).reshape(sent.shape)
    return place_call(moved, rows, width_x, width_y, across, along)


def solution(mesh):
    placed = (P("gx", "gy", None), P(), P(), P(), P("gx", "gy"))
    return jax.shard_map(
        on_device,
        mesh=mesh,
        in_specs=placed,
        out_specs=P(("gx", "gy"), None, None),
        check_vma=False,
    )
```
